32 devices in a mesh: src: 4 (over y, x), dst: 8 (over z, core).
Axes of the slice: x: 2, y: 2, z: 4, core: 2. Of those that a mesh axis runs over, the one named last changes fastest.
Arguments:
- src_emb: float32 [32768, 256], P(('src', 'dst')), may hold values from -2 to 2
- src_acc: float32 [32768], P(('src', 'dst')), may hold values from 0.001 to 0.03
- dst_emb: float32 [16384, 256], P(('src', 'dst')), may hold values from -2 to 2
- dst_acc: float32 [16384], P(('src', 'dst')), may hold values from 0.001 to 0.03
- rel_emb: float32 [128, 256], replicated, may hold values from -4 to 4
- rel_acc: float32 [128], replicated, may hold values from 0.001 to 0.03
- edge_src: int32 [4, 8, 4, 8, 128], P('src', 'dst'), may hold values from 0 to 1023
- edge_dst: int32 [4, 8, 4, 8, 128], P('src', 'dst'), may hold values from 0 to 511
- edge_rel: int32 [4, 8, 4, 8, 128], P('src', 'dst'), may hold values from 0 to 127
- negatives: int32 [4, 8, 4, 8, 128], P('src', 'dst'), may hold values from 0 to 511
Outputs:
- src_out: float32 [32768, 256], P(('src', 'dst'))
- src_acc_out: float32 [32768], P(('src', 'dst'))
- dst_out: float32 [16384, 256], P(('src', 'dst'))
- dst_acc_out: float32 [16384], P(('src', 'dst'))
- rel_out: float32 [128, 256], replicated
- rel_acc_out: float32 [128], replicated
The draws below stay inside these ranges and needn't reach their ends.
All inputs are finite; a program needn't handle non-finite values.
Results may differ from the reference program's by a relative error of at most 0.0003.
Values sent between devices are 32-bit elements; how exact they have to be, the bound alone decides.
No kernel may reach another device: no remote copies, remote signals or barrier semaphores. Data moves between devices by JAX's collectives and lax.ppermute only.
A program may use at most 64 MiB of HBM per device.

```python
import math
import jax
import jax.numpy as jnp
import numpy as np
from jax import lax

D = 256
NREL = 128
NEG = 128
BLOCK_EDGES = 128
EDGE_BLOCKS = 8
STEPS = 4
SRC_ROWS = 1024
DST_ROWS = 512
SRC_TOTAL = 32768
DST_TOTAL = 16384
N_SRC = 4
N_DST = 8


def with_ends(values, rng, least, largest):
    index_at = [jax.random.randint(jax.random.fold_in(rng, axis), (), 0, length) for axis, length in enumerate(values.shape)]
    widest = values.shape.index(max(values.shape))
    neighbour = index_at[:widest] + [(index_at[widest] + 1) % values.shape[widest]] + index_at[widest + 1:]
    return values.at[tuple(index_at)].set(least).at[tuple(neighbour)].set(largest)


def level_of(rng, extent, shards, low, top_value):
    loudness = 1.0
    for position, blocks in shards:
        heights = jax.random.uniform(jax.random.fold_in(jax.random.fold_in(rng, 6), position), (blocks,), jnp.float32, low / len(shards), top_value / len(shards))
        loudness = loudness * jnp.repeat(jnp.exp(heights), extent[position] // blocks).reshape((-1,) + (1,) * (len(extent) - 1 - position))
    return loudness


def rank_table(amount, lean):
    portions = [(1 << 20) // math.isqrt(grade ** lean) + 1 for grade in range(1, amount + 1)]
    scale = 1 + sum(portions) // (1 << 30)
    return np.cumsum(np.array([max(1, weight // scale) for weight in portions]))


def ranked(stream_key, shape, number_of, skew):
    grid = rank_table(number_of, skew)
    pick = jax.random.randint(jax.random.fold_in(stream_key, 1), shape, 0, int(grid[number_of - 1]))
    rank = jnp.searchsorted(jnp.asarray(grid, jnp.int32), pick, side="right")
    return jax.random.permutation(jax.random.fold_in(stream_key, 2), number_of)[rank].astype(jnp.int32)


def normal_values(own_key, dims, scale, reach, shards=(), kind=jnp.bfloat16):
    entries = scale * jax.random.normal(own_key, dims, jnp.float32)
    if shards:
        entries = entries * level_of(own_key, dims, shards, -0.22, 0.18)
    return jnp.clip(entries, -reach, reach).astype(kind)


def setup_inputs(seed: int = 0) -> dict:
    keys = jax.random.split(jax.random.key(seed), 11)
    return {
        "src_emb": normal_values(keys[0], (SRC_TOTAL, D), 0.25, 2.0, ((0, 32),), jnp.float32),
        "src_acc": jnp.clip(jnp.exp(math.log(0.03) - 3.4011973 * jax.random.uniform(keys[1], (SRC_TOTAL,), jnp.float32) ** level_of(keys[1], (SRC_TOTAL,), ((0, 32),), -0.2, 0.2)), 0.001, 0.03),
        "dst_emb": normal_values(keys[2], (DST_TOTAL, D), 0.25, 2.0, ((0, 32),), jnp.float32),
        "dst_acc": jnp.clip(jnp.exp(math.log(0.03) - 3.4011973 * jax.random.uniform(keys[3], (DST_TOTAL,), jnp.float32) ** level_of(keys[3], (DST_TOTAL,), ((0, 32),), -0.2, 0.2)), 0.001, 0.03),
        "rel_emb": normal_values(keys[4], (NREL, D), 1.0, 4.0, (), jnp.float32),
        "rel_acc": jnp.clip(jnp.exp(jax.random.uniform(keys[5], (NREL,), jnp.float32, math.log(0.001), math.log(0.03))), 0.001, 0.03),
        "edge_src": with_ends(jax.random.randint(keys[6], (N_SRC, N_DST, STEPS, EDGE_BLOCKS, BLOCK_EDGES), 0, SRC_ROWS), jax.random.fold_in(keys[6], 1), 0, SRC_ROWS - 1).astype(jnp.int32),
        "edge_dst": with_ends(jax.random.randint(keys[7], (N_SRC, N_DST, STEPS, EDGE_BLOCKS, BLOCK_EDGES), 0, DST_ROWS), jax.random.fold_in(keys[7], 1), 0, DST_ROWS - 1).astype(jnp.int32),
        "edge_rel": with_ends(ranked(keys[8], (N_SRC, N_DST, STEPS, EDGE_BLOCKS, BLOCK_EDGES), NREL, 2), jax.random.fold_in(keys[8], 3), 0, NREL - 1).astype(jnp.int32),
        "negatives": with_ends(jax.random.randint(keys[9], (N_SRC, N_DST, STEPS, EDGE_BLOCKS, NEG), 0, DST_ROWS), jax.random.fold_in(keys[9], 1), 0, DST_ROWS - 1).astype(jnp.int32),
    }


def bucket_grads(src_block, dst_block, rel_emb, src_ids, dst_ids, rel_ids, neg_ids):
    highest = lax.Precision.HIGHEST
    width = src_block.shape[-1]
    onehot = (rel_ids[..., None] == jnp.arange(rel_emb.shape[0], dtype=jnp.int32)).astype(src_block.dtype)
    rel_rows = jnp.einsum('cbr,rd->cbd', onehot, rel_emb, precision=highest)
    src_rows = src_block[src_ids]
    dst_rows = dst_block[dst_ids]
    neg_rows = dst_block[neg_ids]
    query = src_rows * rel_rows
    positive = lax.optimization_barrier(jnp.sum(query * dst_rows, axis=-1))
    scores = jnp.einsum('cbd,ckd->cbk', query, neg_rows, precision=highest)
    pos_weight = -jax.nn.sigmoid(-positive)
    neg_weight = jax.nn.sigmoid(scores) / neg_ids.shape[-1]
    grad_query = pos_weight[..., None] * dst_rows + jnp.einsum('cbk,ckd->cbd', neg_weight, neg_rows, precision=highest)
    grad_dst_pos = pos_weight[..., None] * query
    grad_neg = jnp.einsum('cbk,cbd->ckd', neg_weight, query, precision=highest)
    rel_grad = jnp.einsum('cbr,cbd->rd', onehot, grad_query * src_rows, precision=highest)
    src_grad = jnp.zeros_like(src_block).at[src_ids.reshape(-1)].add((grad_query * rel_rows).reshape(-1, width))
    dst_grad = jnp.zeros_like(dst_block).at[dst_ids.reshape(-1)].add(grad_dst_pos.reshape(-1, width))
    dst_grad = dst_grad.at[neg_ids.reshape(-1)].add(grad_neg.reshape(-1, width))
    return (src_grad, dst_grad, rel_grad)

def adagrad_rows(embedding, summed, grad):
    new_sum = summed + lax.optimization_barrier(jnp.mean(grad * grad, axis=-1))
    return (embedding - 0.3 * grad / (jnp.sqrt(new_sum)[..., None] + 1e-10), new_sum)

def reference(src_emb, src_acc, dst_emb, dst_acc, rel_emb, rel_acc, edge_src, edge_dst, edge_rel, negatives):
    src_blocks = src_emb.reshape(N_SRC, N_DST, SRC_ROWS, D)
    src_sums = src_acc.reshape(N_SRC, N_DST, SRC_ROWS)
    dst_blocks = dst_emb.reshape(N_SRC, N_DST, DST_ROWS, D)
    dst_sums = dst_acc.reshape(N_SRC, N_DST, DST_ROWS)
    relations = rel_emb
    rel_sums = rel_acc
    for step in range(STEPS):
        rolled = jnp.roll(dst_blocks, step, axis=1)

        def per_group(item, relations=relations):

            def one_bucket(src_block, dst_block, src_ids, dst_ids, rel_ids, neg_ids):
                return bucket_grads(src_block, dst_block, relations, src_ids, dst_ids, rel_ids, neg_ids)
            return jax.vmap(one_bucket)(*item)
        src_grad, dst_grad, rel_grad = lax.map(per_group, (src_blocks, rolled, edge_src[:, :, step], edge_dst[:, :, step], edge_rel[:, :, step], negatives[:, :, step]))
        dst_grad = jnp.roll(dst_grad, -step, axis=1)
        src_blocks, src_sums = adagrad_rows(src_blocks, src_sums, src_grad)
        dst_blocks, dst_sums = adagrad_rows(dst_blocks, dst_sums, dst_grad)
        relations, rel_sums = adagrad_rows(relations, rel_sums, lax.optimization_barrier(jnp.sum(rel_grad, axis=(0, 1))))
    return (src_blocks.reshape(-1, D), src_sums.reshape(-1), dst_blocks.reshape(-1, D), dst_sums.reshape(-1), relations, rel_sums)
```

```python
import functools

import jax
import jax.numpy as jnp
from jax import lax
from jax.experimental import pallas as pl
from jax.experimental.pallas import tpu as pltpu
from jax.sharding import PartitionSpec as P

STEPS = 4
RATE = 0.3
EPS = 1e-10
F32 = jnp.float32
BF16 = jnp.bfloat16
LANES = 128
CHUNK = 256


def halves(value):
    high = value.astype(BF16)
    return high, (value - high.astype(F32)).astype(BF16)


def dot(lhs, rhs, lhs_dim=1, rhs_dim=0):
    return lax.dot_general(
        lhs, rhs, (((lhs_dim,), (rhs_dim,)), ((), ())), preferred_element_type=F32
    )


def columns(rows):
    return jnp.transpose(rows)


def hot_columns(cols, first, blocks, width):
    lane = lax.broadcasted_iota(jnp.int32, (LANES, width), 1)
    parts = [
        jnp.where(cols[:, b : b + 1] == lane, 1.0, 0.0).astype(BF16)
        for b in range(first, first + blocks)
    ]
    return jnp.concatenate(parts, axis=0)


def hot_rows(ids, first, blocks, start, height):
    row = lax.broadcasted_iota(jnp.int32, (height, LANES), 0) + start
    parts = [
        jnp.where(row == ids[b : b + 1, :], 1.0, 0.0).astype(BF16)
        for b in range(first, first + blocks)
    ]
    return jnp.concatenate(parts, axis=1)


def row_scale(summed, grad):
    total = summed + jnp.sum(grad * grad, axis=1, keepdims=True) * (1.0 / grad.shape[1])
    return total, RATE / (jnp.sqrt(total) + EPS)


def gather_rows(cols, stack, out_ref, edges, rows):
    blocks = CHUNK // LANES
    for c in range(edges // CHUNK):
        hot = hot_columns(cols, c * blocks, blocks, rows)
        out_ref[c * CHUNK : (c + 1) * CHUNK, :] = dot(jnp.concatenate([hot, hot], axis=1), stack)


def first_kernel(ids_ref, src_ref, out_ref, stack_ref):
    rows = src_ref.shape[0]
    high, low = halves(src_ref[...])
    stack_ref[0:rows, :] = high
    stack_ref[rows : 2 * rows, :] = low
    gather_rows(columns(ids_ref[0]), stack_ref[...], out_ref, out_ref.shape[0], rows)


def count_kernel(neg_ref, out_ref):
    steps, blocks, negs = neg_ref.shape
    rows = out_ref.shape[2]
    for t in range(steps):
        cols = columns(neg_ref[t])
        lane = lax.broadcasted_iota(jnp.int32, (negs, rows), 1)
        parts = [
            jnp.sum(jnp.where(cols[:, b : b + 1] == lane, 1.0 / negs, 0.0), axis=0, keepdims=True)
            for b in range(blocks)
        ]
        out_ref[t] = jnp.concatenate(parts, axis=0)


def relation_update(core_ref, mine_ref, peer_ref, rel_ref, acc_ref):
    first = core_ref[0] == 0
    mine, peer = mine_ref[...], peer_ref[...]
    grad = jnp.concatenate(
        [jnp.where(first, mine, peer), jnp.where(first, peer, mine)], axis=0
    )
    total, scale = row_scale(acc_ref[...], grad)
    return rel_ref[...] - grad * scale, total


def query_kernel(step, updated, *refs):
    if updated:
        core_ref, mine_ref, peer_ref, acc_ref = refs[:4]
        refs = refs[4:]
    else:
        core_ref = refs[0]
        refs = refs[1:]
    rel_ref, src_ref, dst_ref, eds_ref, erl_ref, cnt_ref = refs[:6]
    refs = refs[6:]
    keep_ref, send_ref, wgt_ref, qry_ref, gsr_ref = refs[:5]
    refs = refs[5:]
    if updated:
        rel_out_ref, acc_out_ref = refs
        rel, total = relation_update(core_ref, mine_ref, peer_ref, rel_ref, acc_ref)
        rel_out_ref[...] = rel
        acc_out_ref[...] = total
    else:
        rel = rel_ref[...]
    edges = src_ref.shape[0]
    rows = cnt_ref.shape[2]
    nrel = rel.shape[0]
    blocks = CHUNK // LANES
    rel_stack = jnp.concatenate(halves(rel), axis=0)
    dst_high, dst_low = halves(dst_ref[0:rows, :])
    dst_wide = jnp.concatenate([dst_high, dst_low, dst_high], axis=1)
    dst_tall = jnp.concatenate([dst_high, dst_low, dst_high], axis=0)
    rel_cols = columns(erl_ref[step])
    dst_cols = columns(eds_ref[step])
    lane = lax.broadcasted_iota(jnp.int32, (LANES, rows), 1)
    counts = cnt_ref[step]
    grad = None
    for c in range(edges // CHUNK):
        at = slice(c * CHUNK, (c + 1) * CHUNK)
        hot = hot_columns(rel_cols, c * blocks, blocks, nrel)
        rel_rows = dot(jnp.concatenate([hot, hot], axis=1), rel_stack)
        src_rows = src_ref[at, :]
        query = src_rows * rel_rows
        q_high, q_low = halves(query)
        qry_ref[0, at, :] = q_high
        qry_ref[1, at, :] = q_low
        scores = dot(jnp.concatenate([q_high, q_high, q_low], axis=1), dst_wide, 1, 1)
        chance = 0.5 * jnp.tanh(0.5 * scores) + 0.5
        parts = []
        for b in range(blocks):
            block = c * blocks + b
            part = chance[b * LANES : (b + 1) * LANES, :]
            hit = dst_cols[:, block : block + 1] == lane
            parts.append(part * counts[block : block + 1, :] + jnp.where(hit, part - 1.0, 0.0))
        weight = jnp.concatenate(parts, axis=0)
        w_high, w_low = halves(weight)
        wgt_ref[0, at, :] = w_high
        wgt_ref[1, at, :] = w_low
        grad_query = dot(jnp.concatenate([w_high, w_high, w_low], axis=1), dst_tall)
        g_high, g_low = halves(grad_query * rel_rows)
        gsr_ref[0, at, :] = g_high
        gsr_ref[1, at, :] = g_low
        hot_t = hot_rows(erl_ref[step], c * blocks, blocks, 0, nrel)
        part = dot(
            jnp.concatenate([hot_t, hot_t], axis=1),
            jnp.concatenate(halves(grad_query * src_rows), axis=0),
        )
        grad = part if grad is None else grad + part
    first = core_ref[0] == 0
    half = nrel // 2
    top, bottom = grad[:half], grad[half:]
    keep_ref[...] = jnp.where(first, top, bottom)
    send_ref[...] = jnp.where(first, bottom, top)


def dst_kernel(wgt_ref, qry_ref, dst_ref, out_ref):
    rows = wgt_ref.shape[2]
    width = dst_ref.shape[1]
    grad = (
        dot(wgt_ref[0], qry_ref[0], 0, 0)
        + dot(wgt_ref[0], qry_ref[1], 0, 0)
        + dot(wgt_ref[1], qry_ref[0], 0, 0)
    )
    blocks = rows // LANES
    sums = jnp.concatenate(
        [dst_ref[rows : rows + blocks, 0:LANES], jnp.zeros((8 - blocks, LANES), F32)], axis=0
    ) if blocks < 8 else dst_ref[rows : rows + blocks, 0:LANES]
    cols = columns(sums)
    totals = []
    for b in range(blocks):
        at = slice(b * LANES, (b + 1) * LANES)
        total, scale = row_scale(cols[:, b : b + 1], grad[at])
        out_ref[at, :] = dst_ref[at, :] - grad[at] * scale
        totals.append(total)
    fresh = jnp.transpose(jnp.concatenate(totals + [totals[0]] * (8 - blocks), axis=1))
    out_ref[rows : rows + 8, :] = jnp.concatenate(
        [fresh, jnp.zeros((8, width - LANES), F32)], axis=1
    )


def src_kernel(step, last, esr_ref, gsr_ref, src_ref, acc_ref, *refs):
    if last:
        src_out_ref, acc_out_ref = refs
    else:
        src_out_ref, acc_out_ref, next_ref, stack_ref = refs
    rows = src_ref.shape[0]
    edges = gsr_ref.shape[1]
    gsr = jnp.concatenate([gsr_ref[0], gsr_ref[1]], axis=0)
    cols = columns(acc_ref[...])
    totals = []
    for m in range(rows // CHUNK):
        at = slice(m * CHUNK, (m + 1) * CHUNK)
        hot_t = hot_rows(esr_ref[step], 0, edges // LANES, m * CHUNK, CHUNK)
        grad = dot(jnp.concatenate([hot_t, hot_t], axis=1), gsr)
        summed = jnp.concatenate(
            [
                cols[:, b : b + 1]
                for b in range(m * CHUNK // LANES, (m + 1) * CHUNK // LANES)
            ],
            axis=0,
        )
        total, scale = row_scale(summed, grad)
        fresh = src_ref[at, :] - grad * scale
        src_out_ref[at, :] = fresh
        for b in range(CHUNK // LANES):
            totals.append(total[b * LANES : (b + 1) * LANES])
        if not last:
            high, low = halves(fresh)
            stack_ref[at, :] = high
            stack_ref[rows + m * CHUNK : rows + (m + 1) * CHUNK, :] = low
    acc_out_ref[...] = jnp.transpose(jnp.concatenate(totals, axis=1))
    if not last:
        gather_rows(columns(esr_ref[step + 1]), stack_ref[...], next_ref, edges, rows)


def final_kernel(core_ref, mine_ref, peer_ref, rel_ref, acc_ref, rel_out_ref, acc_out_ref):
    rel, total = relation_update(core_ref, mine_ref, peer_ref, rel_ref, acc_ref)
    rel_out_ref[...] = rel
    acc_out_ref[...] = jnp.transpose(jnp.broadcast_to(total, (total.shape[0], LANES)))[0:1, :]


def call(body, outs, args, scratch=(), smem=0):
    in_specs = [
        pl.BlockSpec(memory_space=pltpu.SMEM if k < smem else pltpu.VMEM)
        for k in range(len(args))
    ]
    return pl.pallas_call(
        body,
        out_shape=tuple(jax.ShapeDtypeStruct(s, d) for s, d in outs),
        in_specs=in_specs,
        out_specs=tuple(pl.BlockSpec(memory_space=pltpu.VMEM) for _ in outs),
        scratch_shapes=list(scratch),
        compiler_params=pltpu.CompilerParams(vmem_limit_bytes=40 << 20),
    )(*args)


def shifted(value, axis, steps):
    count = lax.axis_size(axis)
    return lax.ppermute(value, axis, [(k, (k + steps) % count) for k in range(count)])


def crossed(value, axis, bits):
    count = lax.axis_size(axis)
    return lax.ppermute(value, axis, [(k, k ^ bits) for k in range(count)])


def exchanged(value, axis, low):
    count = lax.axis_size(axis)
    while low < count:
        reach = min(4, count // low)
        value = sum([crossed(value, axis, low * k) for k in range(1, reach)], value)
        low *= reach
    return value


def reduced(keep, send):
    half = keep + crossed(send, "dst", 1)
    half = exchanged(half, "src", 1)
    half = exchanged(half, "dst", 2)
    return half, crossed(half, "dst", 1)


def local(
    src_emb, src_acc, dst_emb, dst_acc, rel_emb, rel_acc, edge_src, edge_dst, edge_rel, negatives
):
    esr, eds, erl, neg = (v[0, 0] for v in (edge_src, edge_dst, edge_rel, negatives))
    steps, eblocks, _ = esr.shape
    edges = eblocks * LANES
    srows, width = src_emb.shape
    drows = dst_emb.shape[0]
    nrel = rel_emb.shape[0]
    core = (lax.axis_index("dst") & 1).astype(jnp.int32).reshape(1)
    src, sacc = src_emb, src_acc.reshape(srows // LANES, LANES)
    dblocks = drows // LANES
    tail = jnp.pad(dst_acc.reshape(dblocks, LANES), ((0, 8 - dblocks), (0, width - LANES)))
    dst = jnp.concatenate([dst_emb, tail], axis=0)
    rel, racc = rel_emb, rel_acc.reshape(nrel, 1)
    stack = pltpu.VMEM((2 * srows, width), BF16)
    (rows,) = call(first_kernel, [((edges, width), F32)], [esr, src], [stack])
    (counts,) = call(count_kernel, [((steps, eblocks, drows), F32)], [neg])
    half = peer = None
    for step in range(steps):
        outs = [
            ((nrel // 2, width), F32),
            ((nrel // 2, width), F32),
            ((2, edges, drows), BF16),
            ((2, edges, width), BF16),
            ((2, edges, width), BF16),
        ]
        if step == 0:
            args = [core, rel, rows, dst, eds, erl, counts]
        else:
            args = [core, half, peer, racc, rel, rows, dst, eds, erl, counts]
            outs += [((nrel, width), F32), ((nrel, 1), F32)]
        res = call(functools.partial(query_kernel, step, step > 0), outs, args, smem=1)
        keep, send, wgt, qry, gsr = res[:5]
        if step > 0:
            rel, racc = res[5:]
        (dst,) = call(dst_kernel, [((drows + 8, width), F32)], [wgt, qry, dst])
        last = step == steps - 1
        dst = shifted(dst, "dst", 1 if not last else -(steps - 1))
        outs = [((srows, width), F32), ((srows // LANES, LANES), F32)]
        if not last:
            outs.append(((edges, width), F32))
        res = call(
            functools.partial(src_kernel, step, last),
            outs,
            [esr, gsr, src, sacc],
            [] if last else [stack],
        )
        src, sacc = res[:2]
        if not last:
            rows = res[2]
        half, peer = reduced(keep, send)
    rel, racc = call(
        final_kernel,
        [((nrel, width), F32), ((1, LANES), F32)],
        [core, half, peer, rel, racc],
        smem=1,
    )
    return (
        src,
        sacc.reshape(-1),
        dst[:drows],
        dst[drows : drows + dblocks, :LANES].reshape(-1),
        rel,
        racc.reshape(-1),
    )


def solution(mesh):
    both = P(("src", "dst"))
    wide = P(("src", "dst"), None)
    edge = P("src", "dst", None, None, None)
    return jax.shard_map(
        local,
        mesh=mesh,
        in_specs=(wide, both, wide, both, P(), P(), edge, edge, edge, edge),
        out_specs=(wide, both, wide, both, P(), P()),
        check_vma=False,
    )
```

```python
import functools

import jax
import jax.numpy as jnp
from jax import lax
from jax.experimental import pallas as pl
from jax.experimental.pallas import tpu as pltpu
from jax.sharding import PartitionSpec as P

STEPS = 4
RATE = 0.3
EPS = 1e-10
F32 = jnp.float32
BF16 = jnp.bfloat16
LANES = 128
CHUNK = 256


def halves(value):
    high = value.astype(BF16)
    return high, (value - high.astype(F32)).astype(BF16)


def dot(lhs, rhs, lhs_dim=1, rhs_dim=0):
    return lax.dot_general(
        lhs, rhs, (((lhs_dim,), (rhs_dim,)), ((), ())), preferred_element_type=F32
    )


def columns(rows):
    return jnp.transpose(rows)


def hot_columns(cols, first, blocks, width):
    lane = lax.broadcasted_iota(jnp.int32, (LANES, width), 1)
    parts = [
        jnp.where(cols[:, b : b + 1] == lane, 1.0, 0.0).astype(BF16)
        for b in range(first, first + blocks)
    ]
    return jnp.concatenate(parts, axis=0)


def hot_rows(ids, first, blocks, start, height):
    row = lax.broadcasted_iota(jnp.int32, (height, LANES), 0) + start
    parts = [
        jnp.where(row == ids[b : b + 1, :], 1.0, 0.0).astype(BF16)
        for b in range(first, first + blocks)
    ]
    return jnp.concatenate(parts, axis=1)


def row_scale(summed, grad):
    total = summed + jnp.sum(grad * grad, axis=1, keepdims=True) * (1.0 / grad.shape[1])
    return total, RATE / (jnp.sqrt(total) + EPS)


def gather_rows(cols, stack, out_ref, edges, rows):
    blocks = CHUNK // LANES
    for c in range(edges // CHUNK):
        hot = hot_columns(cols, c * blocks, blocks, rows)
        out_ref[c * CHUNK : (c + 1) * CHUNK, :] = dot(jnp.concatenate([hot, hot], axis=1), stack)


def write_counts(neg_ref, step, out_ref):
    blocks, negs = neg_ref.shape[1:]
    rows = out_ref.shape[1]
    cols = columns(neg_ref[step])
    lane = lax.broadcasted_iota(jnp.int32, (negs, rows), 1)
    for b in range(blocks):
        hits = jnp.where(cols[:, b : b + 1] == lane, 0.5 / negs, 0.0)
        out_ref[b : b + 1, :] = jnp.sum(hits, axis=0, keepdims=True)


def first_kernel(
    esr_hbm, eds_hbm, erl_hbm, neg_hbm, sac_hbm, dac_hbm, rac_hbm, rel_hbm, src_hbm, dst_hbm,
    esr_ref, eds_ref, erl_ref, neg_ref, sac_ref, rac_ref, rel_ref, src_ref, dst_ref,
    next_ref, cnt_ref, stack_ref, src_sem, sem,
):
    rows = src_ref.shape[0]
    drows, width = dst_hbm.shape
    small = [
        pltpu.make_async_copy(source, target, sem.at[k])
        for k, (source, target) in enumerate(
            [
                (neg_hbm, neg_ref),
                (esr_hbm, esr_ref),
                (dac_hbm, dst_ref.at[pl.ds(drows, dac_hbm.shape[0]), pl.ds(0, LANES)]),
                (dst_hbm, dst_ref.at[pl.ds(0, drows)]),
                (eds_hbm, eds_ref),
                (erl_hbm, erl_ref),
                (sac_hbm, sac_ref),
                (rac_hbm, rac_ref),
                (rel_hbm, rel_ref),
            ]
        )
    ]
    for load in small[:2]:
        load.start()
    chunks = rows // CHUNK
    loads = [
        pltpu.make_async_copy(
            src_hbm.at[pl.ds(m * CHUNK, CHUNK)], src_ref.at[pl.ds(m * CHUNK, CHUNK)], src_sem.at[m]
        )
        for m in range(chunks)
    ]
    for load in loads:
        load.start()
    dst_ref[drows : drows + 8, :] = jnp.zeros((8, width), F32)
    for load in small[2:]:
        load.start()
    small[0].wait()
    write_counts(neg_ref, 0, cnt_ref)
    small[1].wait()
    for m in range(chunks):
        loads[m].wait()
        high, low = halves(src_ref[m * CHUNK : (m + 1) * CHUNK, :])
        stack_ref[m * CHUNK : (m + 1) * CHUNK, :] = high
        stack_ref[rows + m * CHUNK : rows + (m + 1) * CHUNK, :] = low
    gather_rows(columns(esr_ref[0]), stack_ref[...], next_ref, next_ref.shape[0], rows)
    for load in small[2:]:
        load.wait()


def relation_update(core_ref, mine_ref, peer_ref, rel_ref, acc_ref):
    first = core_ref[0] == 0
    mine, peer = mine_ref[...], peer_ref[...]
    grad = jnp.concatenate(
        [jnp.where(first, mine, peer), jnp.where(first, peer, mine)], axis=0
    )
    nrel = grad.shape[0]
    total, scale = row_scale(columns(jnp.broadcast_to(acc_ref[...], (8, nrel)))[:, 0:1], grad)
    return rel_ref[...] - grad * scale, columns(jnp.broadcast_to(total, (nrel, LANES)))[0:1, :]


def query_kernel(step, updated, *refs):
    if updated:
        core_ref, mine_ref, peer_ref, acc_ref = refs[:4]
        refs = refs[4:]
    else:
        core_ref = refs[0]
        refs = refs[1:]
    rel_ref, src_ref, dst_ref, eds_ref, erl_ref, cnt_ref = refs[:6]
    refs = refs[6:]
    keep_ref, send_ref, wgt_ref, qry_ref, gsr_ref = refs[:5]
    refs = refs[5:]
    if updated:
        rel_out_ref, acc_out_ref = refs
        rel, total = relation_update(core_ref, mine_ref, peer_ref, rel_ref, acc_ref)
        rel_out_ref[...] = rel
        acc_out_ref[...] = total
    else:
        rel = rel_ref[...]
    edges = src_ref.shape[0]
    rows = cnt_ref.shape[1]
    nrel = rel.shape[0]
    blocks = CHUNK // LANES
    rel_stack = jnp.concatenate(halves(rel), axis=0)
    dst_high, dst_low = halves(dst_ref[0:rows, :])
    dst_wide = 0.5 * jnp.concatenate([dst_high, dst_low, dst_high], axis=1)
    dst_tall = jnp.concatenate([dst_high, dst_low, dst_high], axis=0)
    rel_cols = columns(erl_ref[step])
    dst_cols = columns(eds_ref[step])
    lane = lax.broadcasted_iota(jnp.int32, (LANES, rows), 1)
    counts = cnt_ref[...]
    grad = None
    for c in range(edges // CHUNK):
        at = slice(c * CHUNK, (c + 1) * CHUNK)
        hot = hot_columns(rel_cols, c * blocks, blocks, nrel)
        rel_rows = dot(jnp.concatenate([hot, hot], axis=1), rel_stack)
        src_rows = src_ref[at, :]
        query = src_rows * rel_rows
        q_high, q_low = halves(query)
        qry_ref[0, at, :] = q_high
        qry_ref[1, at, :] = q_low
        scores = dot(jnp.concatenate([q_high, q_high, q_low], axis=1), dst_wide, 1, 1)
        slope = jnp.tanh(scores)
        parts = []
        for b in range(blocks):
            block = c * blocks + b
            part = slope[b * LANES : (b + 1) * LANES, :]
            hit = jnp.where(dst_cols[:, block : block + 1] == lane, 0.5, 0.0)
            count = counts[block : block + 1, :]
            parts.append(part * (count + hit) + (count - hit))
        weight = jnp.concatenate(parts, axis=0)
        w_high, w_low = halves(weight)
        wgt_ref[0, at, :] = w_high
        wgt_ref[1, at, :] = w_low
        grad_query = dot(jnp.concatenate([w_high, w_high, w_low], axis=1), dst_tall)
        gsr_ref[at, :] = grad_query * rel_rows
        hot_t = hot_rows(erl_ref[step], c * blocks, blocks, 0, nrel)
        part = dot(
            jnp.concatenate([hot_t, hot_t], axis=1),
            jnp.concatenate(halves(grad_query * src_rows), axis=0),
        )
        grad = part if grad is None else grad + part
    first = core_ref[0] == 0
    half = nrel // 2
    top, bottom = grad[:half], grad[half:]
    keep_ref[...] = jnp.where(first, top, bottom)
    send_ref[...] = jnp.where(first, bottom, top)


def dst_kernel(wgt_ref, qry_ref, dst_ref, out_ref, *last):
    rows = wgt_ref.shape[2]
    width = dst_ref.shape[1]
    grad = (
        dot(wgt_ref[0], qry_ref[0], 0, 0)
        + dot(wgt_ref[0], qry_ref[1], 0, 0)
        + dot(wgt_ref[1], qry_ref[0], 0, 0)
    )
    blocks = rows // LANES
    sums = jnp.concatenate(
        [dst_ref[rows : rows + blocks, 0:LANES], jnp.zeros((8 - blocks, LANES), F32)], axis=0
    ) if blocks < 8 else dst_ref[rows : rows + blocks, 0:LANES]
    cols = columns(sums)
    totals = []
    for b in range(blocks):
        at = slice(b * LANES, (b + 1) * LANES)
        total, scale = row_scale(cols[:, b : b + 1], grad[at])
        out_ref[at, :] = dst_ref[at, :] - grad[at] * scale
        totals.append(total)
    fresh = jnp.transpose(jnp.concatenate(totals + [totals[0]] * (8 - blocks), axis=1))
    if last:
        last[0][...] = fresh[0:blocks]
    else:
        out_ref[rows : rows + 8, :] = jnp.concatenate(
            [fresh, jnp.zeros((8, width - LANES), F32)], axis=1
        )


def src_kernel(step, last, esr_ref, neg_ref, gsr_ref, src_ref, acc_ref, *refs):
    if last:
        src_out_ref, acc_out_ref = refs
    else:
        src_out_ref, acc_out_ref, next_ref, cnt_ref, stack_ref = refs
    rows = src_ref.shape[0]
    edges = gsr_ref.shape[0]
    gsr = jnp.concatenate(halves(gsr_ref[...]), axis=0)
    cols = columns(acc_ref[...])
    totals = []
    for m in range(rows // CHUNK):
        at = slice(m * CHUNK, (m + 1) * CHUNK)
        hot_t = hot_rows(esr_ref[step], 0, edges // LANES, m * CHUNK, CHUNK)
        grad = dot(jnp.concatenate([hot_t, hot_t], axis=1), gsr)
        summed = jnp.concatenate(
            [
                cols[:, b : b + 1]
                for b in range(m * CHUNK // LANES, (m + 1) * CHUNK // LANES)
            ],
            axis=0,
        )
        total, scale = row_scale(summed, grad)
        fresh = src_ref[at, :] - grad * scale
        src_out_ref[at, :] = fresh
        for b in range(CHUNK // LANES):
            totals.append(total[b * LANES : (b + 1) * LANES])
        if not last:
            high, low = halves(fresh)
            stack_ref[at, :] = high
            stack_ref[rows + m * CHUNK : rows + (m + 1) * CHUNK, :] = low
    acc_out_ref[...] = jnp.transpose(jnp.concatenate(totals, axis=1))
    if not last:
        gather_rows(columns(esr_ref[step + 1]), stack_ref[...], next_ref, edges, rows)
        write_counts(neg_ref, step + 1, cnt_ref)


def final_kernel(core_ref, mine_ref, peer_ref, rel_ref, acc_ref, rel_out_ref, acc_out_ref):
    rel, total = relation_update(core_ref, mine_ref, peer_ref, rel_ref, acc_ref)
    rel_out_ref[...] = rel
    acc_out_ref[...] = total


def call(body, outs, args, scratch=(), smem=0, hbm=0):
    spaces = [pltpu.SMEM] * smem + [pltpu.VMEM] * (len(args) - smem - hbm) + [pltpu.HBM] * hbm
    in_specs = [pl.BlockSpec(memory_space=space) for space in spaces]
    return pl.pallas_call(
        body,
        out_shape=tuple(jax.ShapeDtypeStruct(s, d) for s, d in outs),
        in_specs=in_specs,
        out_specs=tuple(pl.BlockSpec(memory_space=pltpu.VMEM) for _ in outs),
        scratch_shapes=list(scratch),
        compiler_params=pltpu.CompilerParams(vmem_limit_bytes=40 << 20),
    )(*args[: len(args) - hbm], *[pltpu.with_memory_space_constraint(v, pltpu.HBM) for v in args[len(args) - hbm :]])


def shifted(value, axis, steps):
    count = lax.axis_size(axis)
    return lax.ppermute(value, axis, [(k, (k + steps) % count) for k in range(count)])


def crossed(value, axis, bits):
    count = lax.axis_size(axis)
    return lax.ppermute(value, axis, [(k, k ^ bits) for k in range(count)])


def exchanged(value, axis, low):
    count = lax.axis_size(axis)
    while low < count:
        reach = min(4, count // low)
        value = sum([crossed(value, axis, low * k) for k in range(1, reach)], value)
        low *= reach
    return value


def local(
    src_emb, src_acc, dst_emb, dst_acc, rel_emb, rel_acc, edge_src, edge_dst, edge_rel, negatives
):
    esr, eds, erl, neg = (v[0, 0] for v in (edge_src, edge_dst, edge_rel, negatives))
    steps, eblocks, _ = esr.shape
    edges = eblocks * LANES
    srows, width = src_emb.shape
    drows = dst_emb.shape[0]
    nrel = rel_emb.shape[0]
    core = (lax.axis_index("dst") & 1).astype(jnp.int32).reshape(1)
    sacc = src_acc.reshape(srows // LANES, LANES)
    dblocks = drows // LANES
    stack = pltpu.VMEM((2 * srows, width), BF16)
    ids = (esr.shape, jnp.int32)
    firsts = [
        esr, eds, erl, neg, sacc, dst_acc.reshape(dblocks, LANES), rel_acc.reshape(1, nrel),
        rel_emb, src_emb, dst_emb,
    ]
    esr, eds, erl, neg, sacc, racc, rel, src, dst, rows, counts = call(
        first_kernel,
        [
            ids, ids, ids, ids,
            ((srows // LANES, LANES), F32),
            ((1, nrel), F32),
            ((nrel, width), F32),
            ((srows, width), F32),
            ((drows + 8, width), F32),
            ((edges, width), F32),
            ((eblocks, drows), F32),
        ],
        firsts,
        [stack, pltpu.SemaphoreType.DMA((srows // CHUNK,)), pltpu.SemaphoreType.DMA((len(firsts) - 1,))],
        hbm=len(firsts),
    )
    half = peer = None
    for step in range(steps):
        last = step == steps - 1
        outs = [
            ((nrel // 2, width), F32),
            ((nrel // 2, width), F32),
            ((2, edges, drows), BF16),
            ((2, edges, width), BF16),
            ((edges, width), F32),
        ]
        if step == 0:
            args = [core, rel, rows, dst, eds, erl, counts]
        else:
            args = [core, half, peer, racc, rel, rows, dst, eds, erl, counts]
            outs += [((nrel, width), F32), ((1, nrel), F32)]
        res = call(functools.partial(query_kernel, step, step > 0), outs, args, smem=1)
        keep, send, wgt, qry, gsr = res[:5]
        if step > 0:
            rel, racc = res[5:]
        half = crossed(send, "dst", 1)
        outs = [((drows, width), F32), ((dblocks, LANES), F32)] if last else [((drows + 8, width), F32)]
        res = call(dst_kernel, outs, [wgt, qry, dst])
        half, *res = lax.optimization_barrier((keep + half, *res))
        moved = [shifted(v, "dst", 1 if not last else -(steps - 1)) for v in res]
        half = exchanged(half, "src", 1)
        if last:
            half, gsr = lax.optimization_barrier((half, gsr))
        else:
            half, gsr, moved = lax.optimization_barrier((half, gsr, moved))
        outs = [((srows, width), F32), ((srows // LANES, LANES), F32)]
        if not last:
            outs += [((edges, width), F32), ((eblocks, drows), F32)]
        res = call(
            functools.partial(src_kernel, step, last),
            outs,
            [esr, neg, gsr, src, sacc],
            [] if last else [stack],
        )
        half = exchanged(half, "dst", 2)
        half, *res = lax.optimization_barrier((half, *res))
        peer = crossed(half, "dst", 1)
        src, sacc = res[:2]
        if not last:
            rows, counts = res[2:]
            (dst,) = moved
    rel, racc = call(
        final_kernel,
        [((nrel, width), F32), ((1, nrel), F32)],
        [core, half, peer, rel, racc],
        smem=1,
    )
    return (
        src,
        sacc.reshape(-1),
        moved[0],
        moved[1].reshape(-1),
        rel,
        racc.reshape(-1),
    )


def solution(mesh):
    both = P(("src", "dst"))
    wide = P(("src", "dst"), None)
    edge = P("src", "dst", None, None, None)
    return jax.shard_map(
        local,
        mesh=mesh,
        in_specs=(wide, both, wide, both, P(), P(), edge, edge, edge, edge),
        out_specs=(wide, both, wide, both, P(), P()),
        check_vma=False,
    )
```

```python
import functools

import jax
import jax.numpy as jnp
from jax import lax
from jax.experimental import pallas as pl
from jax.experimental.pallas import tpu as pltpu
from jax.sharding import PartitionSpec as P

STEPS = 4
RATE = 0.3
EPS = 1e-10
F32 = jnp.float32
BF16 = jnp.bfloat16
LANES = 128
CHUNK = 256


def halves(value):
    high = value.astype(BF16)
    return high, (value - high.astype(F32)).astype(BF16)


def dot(lhs, rhs, lhs_dim=1, rhs_dim=0):
    return lax.dot_general(
        lhs, rhs, (((lhs_dim,), (rhs_dim,)), ((), ())), preferred_element_type=F32
    )


def columns(rows):
    return jnp.transpose(rows)


def hot_columns(cols, first, blocks, width):
    lane = lax.broadcasted_iota(jnp.int32, (LANES, width), 1)
    parts = [
        jnp.where(cols[:, b : b + 1] == lane, 1.0, 0.0).astype(BF16)
        for b in range(first, first + blocks)
    ]
    return jnp.concatenate(parts, axis=0)


def hot_rows(ids, first, blocks, start, height):
    row = lax.broadcasted_iota(jnp.int32, (height, LANES), 0) + start
    parts = [
        jnp.where(row == ids[b : b + 1, :], 1.0, 0.0).astype(BF16)
        for b in range(first, first + blocks)
    ]
    return jnp.concatenate(parts, axis=1)


def row_scale(summed, grad):
    total = summed + jnp.sum(grad * grad, axis=1, keepdims=True) * (1.0 / grad.shape[1])
    return total, RATE / (jnp.sqrt(total) + EPS)


def gather_rows(cols, stack, out_ref, edges, rows):
    blocks = CHUNK // LANES
    for c in range(edges // CHUNK):
        hot = hot_columns(cols, c * blocks, blocks, rows)
        out_ref[c * CHUNK : (c + 1) * CHUNK, :] = dot(jnp.concatenate([hot, hot], axis=1), stack)


def write_counts(neg_ref, step, out_ref):
    blocks, negs = neg_ref.shape[1:]
    rows = out_ref.shape[1]
    cols = columns(neg_ref[step])
    lane = lax.broadcasted_iota(jnp.int32, (negs, rows), 1)
    for b in range(blocks):
        hits = jnp.where(cols[:, b : b + 1] == lane, 0.5 / negs, 0.0)
        out_ref[b : b + 1, :] = jnp.sum(hits, axis=0, keepdims=True)


def first_kernel(
    esr_hbm, eds_hbm, erl_hbm, neg_hbm, sac_hbm, dac_hbm, rac_hbm, rel_hbm, src_hbm, dst_hbm,
    esr_ref, eds_ref, erl_ref, neg_ref, sac_ref, rac_ref, rel_ref, src_ref, dst_ref,
    next_ref, cnt_ref, stack_ref, src_sem, sem,
):
    rows = src_ref.shape[0]
    drows, width = dst_hbm.shape
    small = [
        pltpu.make_async_copy(source, target, sem.at[k])
        for k, (source, target) in enumerate(
            [
                (neg_hbm, neg_ref),
                (esr_hbm, esr_ref),
                (dac_hbm, dst_ref.at[pl.ds(drows, dac_hbm.shape[0]), pl.ds(0, LANES)]),
                (dst_hbm, dst_ref.at[pl.ds(0, drows)]),
                (eds_hbm, eds_ref),
                (erl_hbm, erl_ref),
                (sac_hbm, sac_ref),
                (rac_hbm, rac_ref),
                (rel_hbm, rel_ref),
            ]
        )
    ]
    for load in small[:2]:
        load.start()
    chunks = rows // CHUNK
    loads = [
        pltpu.make_async_copy(
            src_hbm.at[pl.ds(m * CHUNK, CHUNK)], src_ref.at[pl.ds(m * CHUNK, CHUNK)], src_sem.at[m]
        )
        for m in range(chunks)
    ]
    for load in loads:
        load.start()
    dst_ref[drows : drows + 8, :] = jnp.zeros((8, width), F32)
    for load in small[2:]:
        load.start()
    small[0].wait()
    write_counts(neg_ref, 0, cnt_ref)
    small[1].wait()
    for m in range(chunks):
        loads[m].wait()
        high, low = halves(src_ref[m * CHUNK : (m + 1) * CHUNK, :])
        stack_ref[m * CHUNK : (m + 1) * CHUNK, :] = high
        stack_ref[rows + m * CHUNK : rows + (m + 1) * CHUNK, :] = low
    gather_rows(columns(esr_ref[0]), stack_ref[...], next_ref, next_ref.shape[0], rows)
    for load in small[2:]:
        load.wait()


def both_halves(core_ref, mine_ref, peer_ref):
    first = core_ref[0] == 0
    mine, peer = mine_ref[...], peer_ref[...]
    return jnp.concatenate([jnp.where(first, mine, peer), jnp.where(first, peer, mine)], axis=0)


def relation_update(grad, rel_ref, acc_ref):
    nrel = grad.shape[0]
    total, scale = row_scale(columns(jnp.broadcast_to(acc_ref[...], (8, nrel)))[:, 0:1], grad)
    return rel_ref[...] - grad * scale, columns(jnp.broadcast_to(total, (nrel, LANES)))[0:1, :]


def query_kernel(step, updated, pieces, *refs):
    spot_ref, *refs = refs
    if updated:
        core_ref, mine_ref, peer_ref, acc_ref = refs[:4]
        refs = refs[4:]
    else:
        core_ref = refs[0]
        refs = refs[1:]
    rel_ref, src_ref, dst_ref, eds_ref, erl_ref, cnt_ref = refs[:6]
    refs = refs[6:]
    keep_ref, send_ref, wgt_ref, qry_ref, gsr_ref = refs[:5]
    refs = refs[5:]
    if updated:
        rel_out_ref, acc_out_ref = refs
        rel, total = relation_update(both_halves(core_ref, mine_ref, peer_ref), rel_ref, acc_ref)
        rel_out_ref[...] = rel
        acc_out_ref[...] = total
    else:
        rel = rel_ref[...]
    edges = src_ref.shape[0]
    rows = cnt_ref.shape[1]
    nrel = rel.shape[0]
    blocks = CHUNK // LANES
    rel_stack = jnp.concatenate(halves(rel), axis=0)
    dst_high, dst_low = halves(dst_ref[0:rows, :])
    dst_wide = 0.5 * jnp.concatenate([dst_high, dst_low, dst_high], axis=1)
    dst_tall = jnp.concatenate([dst_high, dst_low, dst_high], axis=0)
    rel_cols = columns(erl_ref[step])
    dst_cols = columns(eds_ref[step])
    lane = lax.broadcasted_iota(jnp.int32, (LANES, rows), 1)
    counts = cnt_ref[...]
    grad = None
    for c in range(edges // CHUNK):
        at = slice(c * CHUNK, (c + 1) * CHUNK)
        hot = hot_columns(rel_cols, c * blocks, blocks, nrel)
        rel_rows = dot(jnp.concatenate([hot, hot], axis=1), rel_stack)
        src_rows = src_ref[at, :]
        query = src_rows * rel_rows
        q_high, q_low = halves(query)
        qry_ref[0, at, :] = q_high
        qry_ref[1, at, :] = q_low
        scores = dot(jnp.concatenate([q_high, q_high, q_low], axis=1), dst_wide, 1, 1)
        slope = jnp.tanh(scores)
        parts = []
        for b in range(blocks):
            block = c * blocks + b
            part = slope[b * LANES : (b + 1) * LANES, :]
            hit = jnp.where(dst_cols[:, block : block + 1] == lane, 0.5, 0.0)
            count = counts[block : block + 1, :]
            parts.append(part * (count + hit) + (count - hit))
        weight = jnp.concatenate(parts, axis=0)
        w_high, w_low = halves(weight)
        wgt_ref[0, at, :] = w_high
        wgt_ref[1, at, :] = w_low
        grad_query = dot(jnp.concatenate([w_high, w_high, w_low], axis=1), dst_tall)
        gsr_ref[at, :] = grad_query * rel_rows
        hot_t = hot_rows(erl_ref[step], c * blocks, blocks, 0, nrel)
        part = dot(
            jnp.concatenate([hot_t, hot_t], axis=1),
            jnp.concatenate(halves(grad_query * src_rows), axis=0),
        )
        grad = part if grad is None else grad + part
    first = core_ref[0] == 0
    half = nrel // 2
    top, bottom = grad[:half], grad[half:]
    keep = jnp.where(first, top, bottom)
    send = jnp.where(first, bottom, top)
    size = half // pieces
    for m in range(pieces):
        at = pl.ds(pl.multiple_of((spot_ref[0] ^ m) * size, size), size) if pieces > 1 else slice(0, half)
        keep_ref[at, :] = keep[m * size : (m + 1) * size]
        send_ref[at, :] = send[m * size : (m + 1) * size]


def dst_kernel(wgt_ref, qry_ref, dst_ref, *outs):
    rows = wgt_ref.shape[2]
    width = dst_ref.shape[1]
    head = 0 if len(outs) == 1 else outs[0].shape[0]
    tail_ref = outs[-1]
    grad = (
        dot(wgt_ref[0], qry_ref[0], 0, 0)
        + dot(wgt_ref[0], qry_ref[1], 0, 0)
        + dot(wgt_ref[1], qry_ref[0], 0, 0)
    )
    blocks = rows // LANES
    cols = columns(dst_ref[rows : rows + 8, 0:LANES])
    totals = []
    for b in range(blocks):
        at = slice(b * LANES, (b + 1) * LANES)
        total, scale = row_scale(cols[:, b : b + 1], grad[at])
        totals.append(total)
        fresh = dst_ref[at, :] - grad[at] * scale
        if b * LANES < head:
            outs[0][at, :] = fresh
        else:
            tail_ref[b * LANES - head : (b + 1) * LANES - head, :] = fresh
    sums = jnp.transpose(jnp.concatenate(totals + [totals[0]] * (8 - blocks), axis=1))
    tail_ref[rows - head : rows - head + 8, :] = jnp.concatenate(
        [sums, jnp.zeros((8, width - LANES), F32)], axis=1
    )


def src_kernel(step, last, esr_ref, neg_ref, gsr_ref, src_ref, acc_ref, *refs):
    if last:
        src_out_ref, acc_out_ref = refs
    else:
        src_out_ref, acc_out_ref, next_ref, cnt_ref, stack_ref = refs
    rows = src_ref.shape[0]
    edges = gsr_ref.shape[0]
    gsr = jnp.concatenate(halves(gsr_ref[...]), axis=0)
    cols = columns(acc_ref[...])
    totals = []
    for m in range(rows // CHUNK):
        at = slice(m * CHUNK, (m + 1) * CHUNK)
        hot_t = hot_rows(esr_ref[step], 0, edges // LANES, m * CHUNK, CHUNK)
        grad = dot(jnp.concatenate([hot_t, hot_t], axis=1), gsr)
        summed = jnp.concatenate(
            [
                cols[:, b : b + 1]
                for b in range(m * CHUNK // LANES, (m + 1) * CHUNK // LANES)
            ],
            axis=0,
        )
        total, scale = row_scale(summed, grad)
        fresh = src_ref[at, :] - grad * scale
        src_out_ref[at, :] = fresh
        for b in range(CHUNK // LANES):
            totals.append(total[b * LANES : (b + 1) * LANES])
        if not last:
            high, low = halves(fresh)
            stack_ref[at, :] = high
            stack_ref[rows + m * CHUNK : rows + (m + 1) * CHUNK, :] = low
    acc_out_ref[...] = jnp.transpose(jnp.concatenate(totals, axis=1))
    if not last:
        gather_rows(columns(esr_ref[step + 1]), stack_ref[...], next_ref, edges, rows)
        write_counts(neg_ref, step + 1, cnt_ref)


def final_kernel(core_ref, spot_ref, *refs):
    pairs = refs[:-12]
    rel_ref, acc_ref, head_ref, tail_ref = refs[-12:-8]
    rel_out, acc_out, dst_out, dac_out, grad_ref, rel_buf, acc_buf, sem = refs[-8:]
    head = head_ref.shape[0]
    rest = dst_out.shape[0] - head
    moves = [
        pltpu.make_async_copy(source, target, sem.at[k])
        for k, (source, target) in enumerate(
            [
                (head_ref, dst_out.at[pl.ds(0, head)]),
                (tail_ref.at[pl.ds(0, rest)], dst_out.at[pl.ds(head, rest)]),
                (tail_ref.at[pl.ds(rest, dac_out.shape[0]), pl.ds(0, LANES)], dac_out),
                (rel_buf, rel_out),
                (acc_buf, acc_out),
            ]
        )
    ]
    for move in moves[:3]:
        move.start()
    rows = pairs[0].shape[0] // 2
    half = grad_ref.shape[0] // 2
    core = core_ref[0]
    for k, pair_ref in enumerate(pairs):
        at = (spot_ref[0] ^ k) * rows
        mine = pl.multiple_of(core * half + at, rows)
        peer = pl.multiple_of((1 - core) * half + at, rows)
        grad_ref[pl.ds(mine, rows), :] = pair_ref[0:rows, :]
        grad_ref[pl.ds(peer, rows), :] = pair_ref[rows : 2 * rows, :]
    rel, total = relation_update(grad_ref[...], rel_ref, acc_ref)
    rel_buf[...] = rel
    acc_buf[...] = total
    for move in moves[3:]:
        move.start()
    for move in moves:
        move.wait()


def call(body, outs, args, scratch=(), smem=0, hbm=0, out_space=pltpu.VMEM):
    spaces = [pltpu.SMEM] * smem + [pltpu.VMEM] * (len(args) - smem - hbm) + [pltpu.HBM] * hbm
    in_specs = [pl.BlockSpec(memory_space=space) for space in spaces]
    return pl.pallas_call(
        body,
        out_shape=tuple(jax.ShapeDtypeStruct(s, d) for s, d in outs),
        in_specs=in_specs,
        out_specs=tuple(pl.BlockSpec(memory_space=out_space) for _ in outs),
        scratch_shapes=list(scratch),
        compiler_params=pltpu.CompilerParams(vmem_limit_bytes=40 << 20),
    )(*args[: len(args) - hbm], *[pltpu.with_memory_space_constraint(v, pltpu.HBM) for v in args[len(args) - hbm :]])


def shifted(value, axis, steps):
    count = lax.axis_size(axis)
    return lax.ppermute(value, axis, [(k, (k + steps) % count) for k in range(count)])


def crossed(value, axis, bits):
    count = lax.axis_size(axis)
    return lax.ppermute(value, axis, [(k, k ^ bits) for k in range(count)])


def exchanged(value, axis, low, late=None):
    count = lax.axis_size(axis)
    while low < count:
        reach = min(4, count // low)
        last = value
        if late is not None:
            last, late = lax.optimization_barrier((value, late))
        come = [crossed(last if k == 1 else value, axis, low * k) for k in range(1, reach)]
        value = sum(come, value)
        low *= reach
        if late is not None:
            return exchanged(value, axis, low), late
    return value


def local(
    src_emb, src_acc, dst_emb, dst_acc, rel_emb, rel_acc, edge_src, edge_dst, edge_rel, negatives
):
    esr, eds, erl, neg = (v[0, 0] for v in (edge_src, edge_dst, edge_rel, negatives))
    steps, eblocks, _ = esr.shape
    edges = eblocks * LANES
    srows, width = src_emb.shape
    drows = dst_emb.shape[0]
    nrel = rel_emb.shape[0]
    core = (lax.axis_index("dst") & 1).astype(jnp.int32).reshape(1)
    spot = lax.axis_index("src").astype(jnp.int32).reshape(1)
    nsrc = lax.axis_size("src")
    head = (drows // LANES // 2) * LANES
    sacc = src_acc.reshape(srows // LANES, LANES)
    dblocks = drows // LANES
    stack = pltpu.VMEM((2 * srows, width), BF16)
    ids = (esr.shape, jnp.int32)
    firsts = [
        esr, eds, erl, neg, sacc, dst_acc.reshape(dblocks, LANES), rel_acc.reshape(1, nrel),
        rel_emb, src_emb, dst_emb,
    ]
    esr, eds, erl, neg, sacc, racc, rel, src, dst, rows, counts = call(
        first_kernel,
        [
            ids, ids, ids, ids,
            ((srows // LANES, LANES), F32),
            ((1, nrel), F32),
            ((nrel, width), F32),
            ((srows, width), F32),
            ((drows + 8, width), F32),
            ((edges, width), F32),
            ((eblocks, drows), F32),
        ],
        firsts,
        [stack, pltpu.SemaphoreType.DMA((srows // CHUNK,)), pltpu.SemaphoreType.DMA((len(firsts),))],
        hbm=len(firsts),
    )
    half = peer = None
    for step in range(steps):
        last = step == steps - 1
        outs = [
            ((nrel // 2, width), F32),
            ((nrel // 2, width), F32),
            ((2, edges, drows), BF16),
            ((2, edges, width), BF16),
            ((edges, width), F32),
        ]
        if step == 0:
            args = [spot, core, rel, rows, dst, eds, erl, counts]
        else:
            args = [spot, core, half, peer, racc, rel, rows, dst, eds, erl, counts]
            outs += [((nrel, width), F32), ((1, nrel), F32)]
        res = call(functools.partial(query_kernel, step, step > 0, nsrc if last else 1), outs, args, smem=2)
        keep, send, wgt, qry, gsr = res[:5]
        if step > 0:
            rel, racc = res[5:]
        come = crossed(send, "dst", 1)
        parts = [head, drows - head + 8] if last else [drows + 8]
        dst = call(dst_kernel, [((n, width), F32) for n in parts], [wgt, qry, dst])
        come, *dst = lax.optimization_barrier((come, *dst))
        dst = [shifted(v, "dst", -(steps - 1) if last else 1) for v in dst]
        half = keep + come
        outs = [((srows, width), F32), ((srows // LANES, LANES), F32)]
        if last:
            size = nrel // 2 // nsrc
            half = half[:size] + sum(
                crossed(half[k * size : (k + 1) * size], "src", k) for k in range(1, nsrc)
            )
            src, sacc = call(
                functools.partial(src_kernel, step, last), outs, [esr, neg, gsr, src, sacc]
            )
            half, src, sacc, dst[0] = lax.optimization_barrier((half, src, sacc, dst[0]))
            half = exchanged(half, "dst", 2)
            pair = jnp.concatenate([half, crossed(half, "dst", 1)], axis=0)
            pairs = [pair] + [crossed(pair, "src", k) for k in range(1, nsrc)]
        else:
            half = exchanged(half, "src", 1)
            half, gsr = lax.optimization_barrier((half, gsr))
            outs += [((edges, width), F32), ((eblocks, drows), F32)]
            res = call(
                functools.partial(src_kernel, step, last), outs, [esr, neg, gsr, src, sacc], [stack]
            )
            half, (dst,) = exchanged(half, "dst", 2, dst)
            half, src, sacc, rows, counts = lax.optimization_barrier((half, *res))
            peer = crossed(half, "dst", 1)
    rel, racc, dst, dacc = call(
        final_kernel,
        [((nrel, width), F32), ((1, nrel), F32), ((drows, width), F32), ((dblocks, LANES), F32)],
        [core, spot, *pairs, rel, racc, *dst],
        [
            pltpu.VMEM((nrel, width), F32),
            pltpu.VMEM((nrel, width), F32),
            pltpu.VMEM((1, nrel), F32),
            pltpu.SemaphoreType.DMA((5,)),
        ],
        smem=2,
        out_space=pltpu.HBM,
    )
    return src, sacc.reshape(-1), dst, dacc.reshape(-1), rel, racc.reshape(-1)


def solution(mesh):
    both = P(("src", "dst"))
    wide = P(("src", "dst"), None)
    edge = P("src", "dst", None, None, None)
    return jax.shard_map(
        local,
        mesh=mesh,
        in_specs=(wide, both, wide, both, P(), P(), edge, edge, edge, edge),
        out_specs=(wide, both, wide, both, P(), P()),
        check_vma=False,
    )
```

```python
import functools

import jax
import jax.numpy as jnp
from jax import lax
from jax.experimental import pallas as pl
from jax.experimental.pallas import tpu as pltpu
from jax.sharding import PartitionSpec as P

STEPS = 4
RATE = 0.3
EPS = 1e-10
F32 = jnp.float32
BF16 = jnp.bfloat16
LANES = 128
CHUNK = 256
QUERIES = 512


def halves(value):
    high = value.astype(BF16)
    return high, (value - high.astype(F32)).astype(BF16)


def dot(lhs, rhs, lhs_dim=1, rhs_dim=0):
    return lax.dot_general(
        lhs, rhs, (((lhs_dim,), (rhs_dim,)), ((), ())), preferred_element_type=F32
    )


def columns(rows):
    return jnp.transpose(rows)


def hot_columns(cols, first, blocks, width):
    lane = lax.broadcasted_iota(jnp.int32, (LANES, width), 1)
    parts = [
        jnp.where(cols[:, b : b + 1] == lane, 1.0, 0.0).astype(BF16)
        for b in range(first, first + blocks)
    ]
    return jnp.concatenate(parts, axis=0)


def hot_rows(ids, first, blocks, start, height):
    row = lax.broadcasted_iota(jnp.int32, (height, LANES), 0) + start
    parts = [
        jnp.where(row == ids[b : b + 1, :], 1.0, 0.0).astype(BF16)
        for b in range(first, first + blocks)
    ]
    return jnp.concatenate(parts, axis=1)


def row_scale(summed, grad):
    total = summed + jnp.sum(grad * grad, axis=1, keepdims=True) * (1.0 / grad.shape[1])
    return total, RATE / (jnp.sqrt(total) + EPS)


def gather_rows(cols, stack, out_ref, edges, rows):
    blocks = CHUNK // LANES
    for c in range(edges // CHUNK):
        hot = hot_columns(cols, c * blocks, blocks, rows)
        out_ref[c * CHUNK : (c + 1) * CHUNK, :] = dot(jnp.concatenate([hot, hot], axis=1), stack)


def prepare(step, eds_ref, erl_ref, neg_ref, cnt_ref, hit_ref, hot_ref, hot_t_ref):
    blocks, negs = neg_ref.shape[1:]
    rows = cnt_ref.shape[1]
    nrel = hot_t_ref.shape[0]
    cols = columns(neg_ref[step])
    dst_cols = columns(eds_ref[step])
    lane = lax.broadcasted_iota(jnp.int32, (LANES, rows), 1)
    for b in range(blocks):
        found = jnp.where(cols[:, b : b + 1] == lane, 0.5 / negs, 0.0)
        count = jnp.sum(found, axis=0, keepdims=True)
        cnt_ref[b : b + 1, :] = 2.0 * count
        own = jnp.where(dst_cols[:, b : b + 1] == lane, 0.5, 0.0)
        hit_ref[b * LANES : (b + 1) * LANES, :] = own + count
    hot_ref[...] = hot_columns(columns(erl_ref[step]), 0, blocks, nrel)
    hot_t_ref[...] = hot_rows(erl_ref[step], 0, blocks, 0, nrel)


def first_kernel(
    esr_hbm, eds_hbm, erl_hbm, neg_hbm, sac_hbm, dac_hbm, rac_hbm, rel_hbm, src_hbm, dst_hbm,
    esr_ref, eds_ref, erl_ref, neg_ref, sac_ref, rac_ref, rel_ref, src_ref, dst_ref,
    next_ref, cnt_ref, hit_ref, hot_ref, hot_t_ref, stack_ref, src_sem, sem,
):
    rows = src_ref.shape[0]
    drows, width = dst_hbm.shape
    small = [
        pltpu.make_async_copy(source, target, sem.at[k])
        for k, (source, target) in enumerate(
            [
                (neg_hbm, neg_ref),
                (esr_hbm, esr_ref),
                (eds_hbm, eds_ref),
                (erl_hbm, erl_ref),
                (dac_hbm, dst_ref.at[pl.ds(drows, dac_hbm.shape[0]), pl.ds(0, LANES)]),
                (dst_hbm, dst_ref.at[pl.ds(0, drows)]),
                (sac_hbm, sac_ref),
                (rac_hbm, rac_ref),
                (rel_hbm, rel_ref),
            ]
        )
    ]
    for load in small[:4]:
        load.start()
    chunks = rows // CHUNK
    loads = [
        pltpu.make_async_copy(
            src_hbm.at[pl.ds(m * CHUNK, CHUNK)], src_ref.at[pl.ds(m * CHUNK, CHUNK)], src_sem.at[m]
        )
        for m in range(chunks)
    ]
    for load in loads:
        load.start()
    dst_ref[drows : drows + 8, :] = jnp.zeros((8, width), F32)
    for load in small[4:]:
        load.start()
    for load in small[:4]:
        load.wait()
    prepare(0, eds_ref, erl_ref, neg_ref, cnt_ref, hit_ref, hot_ref, hot_t_ref)
    for m in range(chunks):
        loads[m].wait()
        high, low = halves(src_ref[m * CHUNK : (m + 1) * CHUNK, :])
        stack_ref[m * CHUNK : (m + 1) * CHUNK, :] = high
        stack_ref[rows + m * CHUNK : rows + (m + 1) * CHUNK, :] = low
    gather_rows(columns(esr_ref[0]), stack_ref[...], next_ref, next_ref.shape[0], rows)
    for load in small[4:]:
        load.wait()


def both_halves(core_ref, mine_ref, peer_ref):
    first = core_ref[0] == 0
    mine, peer = mine_ref[...], peer_ref[...]
    return jnp.concatenate([jnp.where(first, mine, peer), jnp.where(first, peer, mine)], axis=0)


def relation_update(grad, rel_ref, acc_ref):
    nrel = grad.shape[0]
    total, scale = row_scale(columns(jnp.broadcast_to(acc_ref[...], (8, nrel)))[:, 0:1], grad)
    return rel_ref[...] - grad * scale, columns(jnp.broadcast_to(total, (nrel, LANES)))[0:1, :]


def query_kernel(step, updated, pieces, *refs):
    spot_ref, *refs = refs
    if updated:
        core_ref, mine_ref, peer_ref, acc_ref = refs[:4]
        refs = refs[4:]
    else:
        core_ref = refs[0]
        refs = refs[1:]
    rel_ref, src_ref, dst_ref, cnt_ref, hit_ref, hot_ref, hot_t_ref = refs[:7]
    refs = refs[7:]
    keep_ref, send_ref, wgt_ref, qry_ref, gsr_ref = refs[:5]
    refs = refs[5:]
    if updated:
        rel_out_ref, acc_out_ref = refs
        rel, total = relation_update(both_halves(core_ref, mine_ref, peer_ref), rel_ref, acc_ref)
        rel_out_ref[...] = rel
        acc_out_ref[...] = total
    else:
        rel = rel_ref[...]
    edges = src_ref.shape[0]
    rows = cnt_ref.shape[1]
    nrel = rel.shape[0]
    blocks = QUERIES // LANES
    rel_stack = jnp.concatenate(halves(rel), axis=0)
    dst_high, dst_low = halves(dst_ref[0:rows, :])
    half_high, half_low = 0.5 * dst_high, 0.5 * dst_low
    counts = cnt_ref[...]

    def ask(c):
        at = slice(c * QUERIES, (c + 1) * QUERIES)
        hot = hot_ref[at, :]
        rel_rows = dot(jnp.concatenate([hot, hot], axis=1), rel_stack)
        query = src_ref[at, :] * rel_rows
        q_high, q_low = halves(query)
        qry_ref[0, at, :] = q_high
        qry_ref[1, at, :] = q_low
        scores = (
            dot(q_high, half_high, 1, 1) + dot(q_high, half_low, 1, 1) + dot(q_low, half_high, 1, 1)
        )
        return rel_rows, scores

    def answer(c, rel_rows, scores):
        at = slice(c * QUERIES, (c + 1) * QUERIES)
        slope = jnp.tanh(scores) - 1.0
        parts = []
        for b in range(blocks):
            block = c * blocks + b
            rows_at = slice(block * LANES, (block + 1) * LANES)
            part = slope[b * LANES : (b + 1) * LANES, :]
            parts.append(hit_ref[rows_at, :] * part + counts[block : block + 1, :])
        weight = jnp.concatenate(parts, axis=0)
        w_high, w_low = halves(weight)
        wgt_ref[0, at, :] = w_high
        wgt_ref[1, at, :] = w_low
        grad_query = dot(w_high, dst_high) + dot(w_high, dst_low) + dot(w_low, dst_high)
        gsr_ref[at, :] = grad_query * rel_rows
        return grad_query

    def share(c, grad_query):
        at = slice(c * QUERIES, (c + 1) * QUERIES)
        hot_t = hot_t_ref[:, at]
        return dot(
            jnp.concatenate([hot_t, hot_t], axis=1),
            jnp.concatenate(halves(grad_query * src_ref[at, :]), axis=0),
        )

    count = edges // QUERIES
    grad = None
    asked = ask(0)
    for c in range(count):
        ready = asked
        if c + 1 < count:
            asked = ask(c + 1)
        part = share(c, answer(c, *ready))
        grad = part if grad is None else grad + part
    first = core_ref[0] == 0
    half = nrel // 2
    top, bottom = grad[:half], grad[half:]
    keep = jnp.where(first, top, bottom)
    send = jnp.where(first, bottom, top)
    size = half // pieces
    for m in range(pieces):
        at = pl.ds(pl.multiple_of((spot_ref[0] ^ m) * size, size), size) if pieces > 1 else slice(0, half)
        keep_ref[at, :] = keep[m * size : (m + 1) * size]
        send_ref[at, :] = send[m * size : (m + 1) * size]


def dst_kernel(wgt_ref, qry_ref, dst_ref, *outs):
    rows = wgt_ref.shape[2]
    width = dst_ref.shape[1]
    head = 0 if len(outs) == 1 else outs[0].shape[0]
    tail_ref = outs[-1]
    grad = (
        dot(wgt_ref[0], qry_ref[0], 0, 0)
        + dot(wgt_ref[0], qry_ref[1], 0, 0)
        + dot(wgt_ref[1], qry_ref[0], 0, 0)
    )
    blocks = rows // LANES
    cols = columns(dst_ref[rows : rows + 8, 0:LANES])
    totals = []
    for b in range(blocks):
        at = slice(b * LANES, (b + 1) * LANES)
        total, scale = row_scale(cols[:, b : b + 1], grad[at])
        totals.append(total)
        fresh = dst_ref[at, :] - grad[at] * scale
        if b * LANES < head:
            outs[0][at, :] = fresh
        else:
            tail_ref[b * LANES - head : (b + 1) * LANES - head, :] = fresh
    sums = jnp.transpose(jnp.concatenate(totals + [totals[0]] * (8 - blocks), axis=1))
    tail_ref[rows - head : rows - head + 8, :] = jnp.concatenate(
        [sums, jnp.zeros((8, width - LANES), F32)], axis=1
    )


def src_kernel(step, last, esr_ref, eds_ref, erl_ref, neg_ref, gsr_ref, src_ref, acc_ref, *refs):
    if last:
        src_out_ref, acc_out_ref = refs
    else:
        src_out_ref, acc_out_ref, next_ref, *prep, stack_ref = refs
    rows = src_ref.shape[0]
    edges = gsr_ref.shape[0]
    gsr = jnp.concatenate(halves(gsr_ref[...]), axis=0)
    cols = columns(acc_ref[...])
    totals = []
    for m in range(rows // CHUNK):
        at = slice(m * CHUNK, (m + 1) * CHUNK)
        hot_t = hot_rows(esr_ref[step], 0, edges // LANES, m * CHUNK, CHUNK)
        grad = dot(jnp.concatenate([hot_t, hot_t], axis=1), gsr)
        summed = jnp.concatenate(
            [
                cols[:, b : b + 1]
                for b in range(m * CHUNK // LANES, (m + 1) * CHUNK // LANES)
            ],
            axis=0,
        )
        total, scale = row_scale(summed, grad)
        fresh = src_ref[at, :] - grad * scale
        src_out_ref[at, :] = fresh
        for b in range(CHUNK // LANES):
            totals.append(total[b * LANES : (b + 1) * LANES])
        if not last:
            high, low = halves(fresh)
            stack_ref[at, :] = high
            stack_ref[rows + m * CHUNK : rows + (m + 1) * CHUNK, :] = low
    acc_out_ref[...] = jnp.transpose(jnp.concatenate(totals, axis=1))
    if not last:
        gather_rows(columns(esr_ref[step + 1]), stack_ref[...], next_ref, edges, rows)
        prepare(step + 1, eds_ref, erl_ref, neg_ref, *prep)


def final_kernel(core_ref, spot_ref, *refs):
    pairs = refs[:-12]
    rel_ref, acc_ref, head_ref, tail_ref = refs[-12:-8]
    rel_out, acc_out, dst_out, dac_out, grad_ref, rel_buf, acc_buf, sem = refs[-8:]
    head = head_ref.shape[0]
    rest = dst_out.shape[0] - head
    moves = [
        pltpu.make_async_copy(source, target, sem.at[k])
        for k, (source, target) in enumerate(
            [
                (head_ref, dst_out.at[pl.ds(0, head)]),
                (tail_ref.at[pl.ds(0, rest)], dst_out.at[pl.ds(head, rest)]),
                (tail_ref.at[pl.ds(rest, dac_out.shape[0]), pl.ds(0, LANES)], dac_out),
                (rel_buf, rel_out),
                (acc_buf, acc_out),
            ]
        )
    ]
    for move in moves[:3]:
        move.start()
    rows = pairs[0].shape[0] // 2
    half = grad_ref.shape[0] // 2
    core = core_ref[0]
    for k, pair_ref in enumerate(pairs):
        at = (spot_ref[0] ^ k) * rows
        mine = pl.multiple_of(core * half + at, rows)
        peer = pl.multiple_of((1 - core) * half + at, rows)
        grad_ref[pl.ds(mine, rows), :] = pair_ref[0:rows, :]
        grad_ref[pl.ds(peer, rows), :] = pair_ref[rows : 2 * rows, :]
    rel, total = relation_update(grad_ref[...], rel_ref, acc_ref)
    rel_buf[...] = rel
    acc_buf[...] = total
    for move in moves[3:]:
        move.start()
    for move in moves:
        move.wait()


def call(body, outs, args, scratch=(), smem=0, hbm=0, out_space=pltpu.VMEM):
    spaces = [pltpu.SMEM] * smem + [pltpu.VMEM] * (len(args) - smem - hbm) + [pltpu.HBM] * hbm
    in_specs = [pl.BlockSpec(memory_space=space) for space in spaces]
    return pl.pallas_call(
        body,
        out_shape=tuple(jax.ShapeDtypeStruct(s, d) for s, d in outs),
        in_specs=in_specs,
        out_specs=tuple(pl.BlockSpec(memory_space=out_space) for _ in outs),
        scratch_shapes=list(scratch),
        compiler_params=pltpu.CompilerParams(vmem_limit_bytes=40 << 20),
    )(*args[: len(args) - hbm], *[pltpu.with_memory_space_constraint(v, pltpu.HBM) for v in args[len(args) - hbm :]])


def shifted(value, axis, steps):
    count = lax.axis_size(axis)
    return lax.ppermute(value, axis, [(k, (k + steps) % count) for k in range(count)])


def crossed(value, axis, bits):
    count = lax.axis_size(axis)
    return lax.ppermute(value, axis, [(k, k ^ bits) for k in range(count)])


def exchanged(value, axis, low, late=None):
    count = lax.axis_size(axis)
    while low < count:
        reach = min(4, count // low)
        last = value
        if late is not None:
            last, late = lax.optimization_barrier((value, late))
        come = [crossed(last if k == 1 else value, axis, low * k) for k in range(1, reach)]
        value = sum(come, value)
        low *= reach
        if late is not None:
            return exchanged(value, axis, low), late
    return value


def local(
    src_emb, src_acc, dst_emb, dst_acc, rel_emb, rel_acc, edge_src, edge_dst, edge_rel, negatives
):
    esr, eds, erl, neg = (v[0, 0] for v in (edge_src, edge_dst, edge_rel, negatives))
    steps, eblocks, _ = esr.shape
    edges = eblocks * LANES
    srows, width = src_emb.shape
    drows = dst_emb.shape[0]
    nrel = rel_emb.shape[0]
    core = (lax.axis_index("dst") & 1).astype(jnp.int32).reshape(1)
    spot = lax.axis_index("src").astype(jnp.int32).reshape(1)
    nsrc = lax.axis_size("src")
    head = (drows // LANES // 2) * LANES
    sacc = src_acc.reshape(srows // LANES, LANES)
    dblocks = drows // LANES
    stack = pltpu.VMEM((2 * srows, width), BF16)
    ids = (esr.shape, jnp.int32)
    prep_shapes = [
        ((eblocks, drows), F32),
        ((edges, drows), F32),
        ((edges, nrel), BF16),
        ((nrel, edges), BF16),
    ]
    firsts = [
        esr, eds, erl, neg, sacc, dst_acc.reshape(dblocks, LANES), rel_acc.reshape(1, nrel),
        rel_emb, src_emb, dst_emb,
    ]
    esr, eds, erl, neg, sacc, racc, rel, src, dst, rows, *prep = call(
        first_kernel,
        [
            ids, ids, ids, ids,
            ((srows // LANES, LANES), F32),
            ((1, nrel), F32),
            ((nrel, width), F32),
            ((srows, width), F32),
            ((drows + 8, width), F32),
            ((edges, width), F32),
            *prep_shapes,
        ],
        firsts,
        [stack, pltpu.SemaphoreType.DMA((srows // CHUNK,)), pltpu.SemaphoreType.DMA((len(firsts),))],
        hbm=len(firsts),
    )
    half = peer = None
    for step in range(steps):
        last = step == steps - 1
        outs = [
            ((nrel // 2, width), F32),
            ((nrel // 2, width), F32),
            ((2, edges, drows), BF16),
            ((2, edges, width), BF16),
            ((edges, width), F32),
        ]
        if step == 0:
            args = [spot, core, rel, rows, dst, *prep]
        else:
            args = [spot, core, half, peer, racc, rel, rows, dst, *prep]
            outs += [((nrel, width), F32), ((1, nrel), F32)]
        res = call(functools.partial(query_kernel, step, step > 0, nsrc if last else 1), outs, args, smem=2)
        keep, send, wgt, qry, gsr = res[:5]
        if step > 0:
            rel, racc = res[5:]
        come = crossed(send, "dst", 1)
        parts = [head, drows - head + 8] if last else [drows + 8]
        dst = call(dst_kernel, [((n, width), F32) for n in parts], [wgt, qry, dst])
        come, *dst = lax.optimization_barrier((come, *dst))
        dst = [shifted(v, "dst", -(steps - 1) if last else 1) for v in dst]
        half = keep + come
        outs = [((srows, width), F32), ((srows // LANES, LANES), F32)]
        if last:
            size = nrel // 2 // nsrc
            half = half[:size] + sum(
                crossed(half[k * size : (k + 1) * size], "src", k) for k in range(1, nsrc)
            )
            src, sacc = call(
                functools.partial(src_kernel, step, last), outs, [esr, eds, erl, neg, gsr, src, sacc]
            )
            half, src, sacc, dst[0] = lax.optimization_barrier((half, src, sacc, dst[0]))
            half = exchanged(half, "dst", 2)
            pair = jnp.concatenate([half, crossed(half, "dst", 1)], axis=0)
            pairs = [pair] + [crossed(pair, "src", k) for k in range(1, nsrc)]
        else:
            half = exchanged(half, "src", 1)
            half, gsr = lax.optimization_barrier((half, gsr))
            outs += [((edges, width), F32), *prep_shapes]
            res = call(
                functools.partial(src_kernel, step, last), outs, [esr, eds, erl, neg, gsr, src, sacc], [stack]
            )
            half, (dst,) = exchanged(half, "dst", 2, dst)
            half, src, sacc, rows, *prep = lax.optimization_barrier((half, *res))
            peer = crossed(half, "dst", 1)
    rel, racc, dst, dacc = call(
        final_kernel,
        [((nrel, width), F32), ((1, nrel), F32), ((drows, width), F32), ((dblocks, LANES), F32)],
        [core, spot, *pairs, rel, racc, *dst],
        [
            pltpu.VMEM((nrel, width), F32),
            pltpu.VMEM((nrel, width), F32),
            pltpu.VMEM((1, nrel), F32),
            pltpu.SemaphoreType.DMA((5,)),
        ],
        smem=2,
        out_space=pltpu.HBM,
    )
    return src, sacc.reshape(-1), dst, dacc.reshape(-1), rel, racc.reshape(-1)


def solution(mesh):
    both = P(("src", "dst"))
    wide = P(("src", "dst"), None)
    edge = P("src", "dst", None, None, None)
    return jax.shard_map(
        local,
        mesh=mesh,
        in_specs=(wide, both, wide, both, P(), P(), edge, edge, edge, edge),
        out_specs=(wide, both, wide, both, P(), P()),
        check_vma=False,
    )
```

```python
import functools

import jax
import jax.numpy as jnp
from jax import lax
from jax.experimental import pallas as pl
from jax.experimental.pallas import tpu as pltpu
from jax.sharding import PartitionSpec as P

STEPS = 4
RATE = 0.3
EPS = 1e-10
F32 = jnp.float32
BF16 = jnp.bfloat16
LANES = 128
CHUNK = 256
QUERIES = 512


def halves(value):
    high = value.astype(BF16)
    return high, (value - high.astype(F32)).astype(BF16)


def dot(lhs, rhs, lhs_dim=1, rhs_dim=0):
    return lax.dot_general(
        lhs, rhs, (((lhs_dim,), (rhs_dim,)), ((), ())), preferred_element_type=F32
    )


def columns(rows):
    return jnp.transpose(rows)


def hot_columns(cols, first, blocks, width):
    lane = lax.broadcasted_iota(jnp.int32, (LANES, width), 1)
    parts = [
        jnp.where(cols[:, b : b + 1] == lane, 1.0, 0.0).astype(BF16)
        for b in range(first, first + blocks)
    ]
    return jnp.concatenate(parts, axis=0)


def hot_rows(ids, first, blocks, start, height):
    row = lax.broadcasted_iota(jnp.int32, (height, LANES), 0) + start
    parts = [
        jnp.where(row == ids[b : b + 1, :], 1.0, 0.0).astype(BF16)
        for b in range(first, first + blocks)
    ]
    return jnp.concatenate(parts, axis=1)


def row_scale(summed, grad):
    total = summed + jnp.sum(grad * grad, axis=1, keepdims=True) * (1.0 / grad.shape[1])
    return total, RATE / (jnp.sqrt(total) + EPS)


def gather_rows(cols, stack, out_ref, edges, rows):
    blocks = CHUNK // LANES
    for c in range(edges // CHUNK):
        hot = hot_columns(cols, c * blocks, blocks, rows)
        out_ref[c * CHUNK : (c + 1) * CHUNK, :] = dot(jnp.concatenate([hot, hot], axis=1), stack)


def prepare(step, eds_ref, erl_ref, neg_ref, cnt_ref, hit_ref, hot_ref, hot_t_ref):
    blocks, negs = neg_ref.shape[1:]
    rows = cnt_ref.shape[1]
    nrel = hot_t_ref.shape[0]
    cols = columns(neg_ref[step])
    dst_cols = columns(eds_ref[step])
    lane = lax.broadcasted_iota(jnp.int32, (LANES, rows), 1)
    for b in range(blocks):
        found = jnp.where(cols[:, b : b + 1] == lane, 0.5 / negs, 0.0)
        count = jnp.sum(found, axis=0, keepdims=True)
        cnt_ref[b : b + 1, :] = 2.0 * count
        own = jnp.where(dst_cols[:, b : b + 1] == lane, 0.5, 0.0)
        hit_ref[b * LANES : (b + 1) * LANES, :] = own + count
    hot_ref[...] = hot_columns(columns(erl_ref[step]), 0, blocks, nrel)
    hot_t_ref[...] = hot_rows(erl_ref[step], 0, blocks, 0, nrel)


def first_kernel(
    esr_hbm, eds_hbm, erl_hbm, neg_hbm, sac_hbm, dac_hbm, rac_hbm, rel_hbm, src_hbm, dst_hbm,
    esr_ref, eds_ref, erl_ref, neg_ref, sac_ref, rac_ref, rel_ref, src_ref, dst_ref,
    next_ref, cnt_ref, hit_ref, hot_ref, hot_t_ref, stack_ref, src_sem, sem,
):
    rows = src_ref.shape[0]
    drows, width = dst_hbm.shape
    small = [
        pltpu.make_async_copy(source, target, sem.at[k])
        for k, (source, target) in enumerate(
            [
                (neg_hbm, neg_ref),
                (esr_hbm, esr_ref),
                (eds_hbm, eds_ref),
                (erl_hbm, erl_ref),
                (dac_hbm, dst_ref.at[pl.ds(drows, dac_hbm.shape[0]), pl.ds(0, LANES)]),
                (dst_hbm, dst_ref.at[pl.ds(0, drows)]),
                (sac_hbm, sac_ref),
                (rac_hbm, rac_ref),
                (rel_hbm, rel_ref),
            ]
        )
    ]
    for load in small[:4]:
        load.start()
    chunks = rows // CHUNK
    loads = [
        pltpu.make_async_copy(
            src_hbm.at[pl.ds(m * CHUNK, CHUNK)], src_ref.at[pl.ds(m * CHUNK, CHUNK)], src_sem.at[m]
        )
        for m in range(chunks)
    ]
    for load in loads:
        load.start()
    dst_ref[drows : drows + 8, :] = jnp.zeros((8, width), F32)
    for load in small[4:]:
        load.start()
    for load in small[:4]:
        load.wait()
    prepare(0, eds_ref, erl_ref, neg_ref, cnt_ref, hit_ref, hot_ref, hot_t_ref)
    for m in range(chunks):
        loads[m].wait()
        high, low = halves(src_ref[m * CHUNK : (m + 1) * CHUNK, :])
        stack_ref[m * CHUNK : (m + 1) * CHUNK, :] = high
        stack_ref[rows + m * CHUNK : rows + (m + 1) * CHUNK, :] = low
    gather_rows(columns(esr_ref[0]), stack_ref[...], next_ref, next_ref.shape[0], rows)
    for load in small[4:]:
        load.wait()


def both_halves(core_ref, mine_ref, peer_ref):
    first = core_ref[0] == 0
    mine, peer = mine_ref[...], peer_ref[...]
    return jnp.concatenate([jnp.where(first, mine, peer), jnp.where(first, peer, mine)], axis=0)


def relation_update(grad, rel_ref, acc_ref):
    nrel = grad.shape[0]
    total, scale = row_scale(columns(jnp.broadcast_to(acc_ref[...], (8, nrel)))[:, 0:1], grad)
    return rel_ref[...] - grad * scale, columns(jnp.broadcast_to(total, (nrel, LANES)))[0:1, :]


def query_kernel(step, updated, pieces, *refs):
    spot_ref, *refs = refs
    if updated:
        core_ref, mine_ref, peer_ref, acc_ref = refs[:4]
        refs = refs[4:]
    else:
        core_ref = refs[0]
        refs = refs[1:]
    rel_ref, src_ref, dst_ref, cnt_ref, hit_ref, hot_ref, hot_t_ref = refs[:7]
    refs = refs[7:]
    keep_ref, send_ref, wgt_ref, qry_ref, gsr_ref = refs[:5]
    refs = refs[5:]
    if updated:
        rel_out_ref, acc_out_ref = refs
        rel, total = relation_update(both_halves(core_ref, mine_ref, peer_ref), rel_ref, acc_ref)
        rel_out_ref[...] = rel
        acc_out_ref[...] = total
    else:
        rel = rel_ref[...]
    edges = src_ref.shape[0]
    rows = cnt_ref.shape[1]
    nrel = rel.shape[0]
    blocks = QUERIES // LANES
    rel_stack = jnp.concatenate(halves(rel), axis=0)
    dst_high, dst_low = halves(dst_ref[0:rows, :])
    half_high, half_low = 0.5 * dst_high, 0.5 * dst_low
    counts = cnt_ref[...]

    def ask(c):
        at = slice(c * QUERIES, (c + 1) * QUERIES)
        hot = hot_ref[at, :]
        rel_rows = dot(jnp.concatenate([hot, hot], axis=1), rel_stack)
        query = src_ref[at, :] * rel_rows
        q_high, q_low = halves(query)
        qry_ref[0, at, :] = q_high
        qry_ref[1, at, :] = q_low
        scores = (
            dot(q_high, half_high, 1, 1) + dot(q_high, half_low, 1, 1) + dot(q_low, half_high, 1, 1)
        )
        return rel_rows, scores

    def answer(c, rel_rows, scores):
        at = slice(c * QUERIES, (c + 1) * QUERIES)
        slope = jnp.tanh(scores) - 1.0
        parts = []
        for b in range(blocks):
            block = c * blocks + b
            rows_at = slice(block * LANES, (block + 1) * LANES)
            part = slope[b * LANES : (b + 1) * LANES, :]
            parts.append(hit_ref[rows_at, :] * part + counts[block : block + 1, :])
        weight = jnp.concatenate(parts, axis=0)
        w_high, w_low = halves(weight)
        wgt_ref[0, at, :] = w_high
        wgt_ref[1, at, :] = w_low
        grad_query = dot(w_high, dst_high) + dot(w_high, dst_low) + dot(w_low, dst_high)
        gsr_ref[at, :] = grad_query * rel_rows
        return grad_query

    def share(c, grad_query):
        at = slice(c * QUERIES, (c + 1) * QUERIES)
        hot_t = hot_t_ref[:, at]
        return dot(
            jnp.concatenate([hot_t, hot_t], axis=1),
            jnp.concatenate(halves(grad_query * src_ref[at, :]), axis=0),
        )

    count = edges // QUERIES
    grad = None
    asked = ask(0)
    for c in range(count):
        ready = asked
        if c + 1 < count:
            asked = ask(c + 1)
        part = share(c, answer(c, *ready))
        grad = part if grad is None else grad + part
    first = core_ref[0] == 0
    half = nrel // 2
    top, bottom = grad[:half], grad[half:]
    keep = jnp.where(first, top, bottom)
    send = jnp.where(first, bottom, top)
    size = half // pieces
    for m in range(pieces):
        at = pl.ds(pl.multiple_of((spot_ref[0] ^ m) * size, size), size) if pieces > 1 else slice(0, half)
        keep_ref[at, :] = keep[m * size : (m + 1) * size]
        send_ref[at, :] = send[m * size : (m + 1) * size]


def dst_kernel(wgt_ref, qry_ref, dst_ref, *outs):
    rows = wgt_ref.shape[2]
    width = dst_ref.shape[1]
    head = 0 if len(outs) == 1 else outs[0].shape[0]
    tail_ref = outs[-1]
    grad = (
        dot(wgt_ref[0], qry_ref[0], 0, 0)
        + dot(wgt_ref[0], qry_ref[1], 0, 0)
        + dot(wgt_ref[1], qry_ref[0], 0, 0)
    )
    blocks = rows // LANES
    cols = columns(dst_ref[rows : rows + 8, 0:LANES])
    totals = []
    for b in range(blocks):
        at = slice(b * LANES, (b + 1) * LANES)
        total, scale = row_scale(cols[:, b : b + 1], grad[at])
        totals.append(total)
        fresh = dst_ref[at, :] - grad[at] * scale
        if b * LANES < head:
            outs[0][at, :] = fresh
        else:
            tail_ref[b * LANES - head : (b + 1) * LANES - head, :] = fresh
    sums = jnp.transpose(jnp.concatenate(totals + [totals[0]] * (8 - blocks), axis=1))
    tail_ref[rows - head : rows - head + 8, :] = jnp.concatenate(
        [sums, jnp.zeros((8, width - LANES), F32)], axis=1
    )


def src_kernel(step, last, esr_ref, eds_ref, erl_ref, neg_ref, gsr_ref, src_ref, acc_ref, *refs):
    if last:
        src_out_ref, acc_out_ref = refs
    else:
        src_out_ref, acc_out_ref, next_ref, *prep, stack_ref = refs
    rows = src_ref.shape[0]
    edges = gsr_ref.shape[0]
    gsr = jnp.concatenate(halves(gsr_ref[...]), axis=0)
    cols = columns(acc_ref[...])
    totals = []
    for m in range(rows // CHUNK):
        at = slice(m * CHUNK, (m + 1) * CHUNK)
        hot_t = hot_rows(esr_ref[step], 0, edges // LANES, m * CHUNK, CHUNK)
        grad = dot(jnp.concatenate([hot_t, hot_t], axis=1), gsr)
        summed = jnp.concatenate(
            [
                cols[:, b : b + 1]
                for b in range(m * CHUNK // LANES, (m + 1) * CHUNK // LANES)
            ],
            axis=0,
        )
        total, scale = row_scale(summed, grad)
        fresh = src_ref[at, :] - grad * scale
        src_out_ref[at, :] = fresh
        for b in range(CHUNK // LANES):
            totals.append(total[b * LANES : (b + 1) * LANES])
        if not last:
            high, low = halves(fresh)
            stack_ref[at, :] = high
            stack_ref[rows + m * CHUNK : rows + (m + 1) * CHUNK, :] = low
    acc_out_ref[...] = jnp.transpose(jnp.concatenate(totals, axis=1))
    if not last:
        gather_rows(columns(esr_ref[step + 1]), stack_ref[...], next_ref, edges, rows)
        prepare(step + 1, eds_ref, erl_ref, neg_ref, *prep)


def final_kernel(core_ref, spot_ref, *refs):
    pairs = refs[:-12]
    rel_ref, acc_ref, head_ref, tail_ref = refs[-12:-8]
    rel_out, acc_out, dst_out, dac_out, grad_ref, rel_buf, acc_buf, sem = refs[-8:]
    head = head_ref.shape[0]
    rest = dst_out.shape[0] - head
    moves = [
        pltpu.make_async_copy(source, target, sem.at[k])
        for k, (source, target) in enumerate(
            [
                (head_ref, dst_out.at[pl.ds(0, head)]),
                (tail_ref.at[pl.ds(0, rest)], dst_out.at[pl.ds(head, rest)]),
                (tail_ref.at[pl.ds(rest, dac_out.shape[0]), pl.ds(0, LANES)], dac_out),
                (rel_buf, rel_out),
                (acc_buf, acc_out),
            ]
        )
    ]
    for move in moves[:3]:
        move.start()
    rows = pairs[0].shape[0] // 2
    half = grad_ref.shape[0] // 2
    core = core_ref[0]
    for k, pair_ref in enumerate(pairs):
        at = (spot_ref[0] ^ k) * rows
        mine = pl.multiple_of(core * half + at, rows)
        peer = pl.multiple_of((1 - core) * half + at, rows)
        grad_ref[pl.ds(mine, rows), :] = pair_ref[0:rows, :]
        grad_ref[pl.ds(peer, rows), :] = pair_ref[rows : 2 * rows, :]
    rel, total = relation_update(grad_ref[...], rel_ref, acc_ref)
    rel_buf[...] = rel
    acc_buf[...] = total
    for move in moves[3:]:
        move.start()
    for move in moves:
        move.wait()


def call(body, outs, args, scratch=(), smem=0, hbm=0, out_space=pltpu.VMEM):
    spaces = [pltpu.SMEM] * smem + [pltpu.VMEM] * (len(args) - smem - hbm) + [pltpu.HBM] * hbm
    in_specs = [pl.BlockSpec(memory_space=space) for space in spaces]
    return pl.pallas_call(
        body,
        out_shape=tuple(jax.ShapeDtypeStruct(s, d) for s, d in outs),
        in_specs=in_specs,
        out_specs=tuple(pl.BlockSpec(memory_space=out_space) for _ in outs),
        scratch_shapes=list(scratch),
        compiler_params=pltpu.CompilerParams(vmem_limit_bytes=40 << 20),
    )(*args[: len(args) - hbm], *[pltpu.with_memory_space_constraint(v, pltpu.HBM) for v in args[len(args) - hbm :]])


def shifted(value, axis, steps):
    count = lax.axis_size(axis)
    return lax.ppermute(value, axis, [(k, (k + steps) % count) for k in range(count)])


def crossed(value, axis, bits):
    count = lax.axis_size(axis)
    return lax.ppermute(value, axis, [(k, k ^ bits) for k in range(count)])


def exchanged(value, axis, low, late=None):
    count = lax.axis_size(axis)
    while low < count:
        reach = min(4, count // low)
        last = value
        if late is not None:
            last, late = lax.optimization_barrier((value, late))
        come = [crossed(last if k == 1 else value, axis, low * k) for k in range(1, reach)]
        value = sum(come, value)
        low *= reach
        if late is not None:
            return exchanged(value, axis, low), late
    return value


def local(
    src_emb, src_acc, dst_emb, dst_acc, rel_emb, rel_acc, edge_src, edge_dst, edge_rel, negatives
):
    esr, eds, erl, neg = (v[0, 0] for v in (edge_src, edge_dst, edge_rel, negatives))
    steps, eblocks, _ = esr.shape
    edges = eblocks * LANES
    srows, width = src_emb.shape
    drows = dst_emb.shape[0]
    nrel = rel_emb.shape[0]
    core = (lax.axis_index("dst") & 1).astype(jnp.int32).reshape(1)
    spot = lax.axis_index("src").astype(jnp.int32).reshape(1)
    nsrc = lax.axis_size("src")
    head = (drows // LANES // 2) * LANES
    sacc = src_acc.reshape(srows // LANES, LANES)
    dblocks = drows // LANES
    stack = pltpu.VMEM((2 * srows, width), BF16)
    ids = (esr.shape, jnp.int32)
    prep_shapes = [
        ((eblocks, drows), F32),
        ((edges, drows), F32),
        ((edges, nrel), BF16),
        ((nrel, edges), BF16),
    ]
    firsts = [
        esr, eds, erl, neg, sacc, dst_acc.reshape(dblocks, LANES), rel_acc.reshape(1, nrel),
        rel_emb, src_emb, dst_emb,
    ]
    esr, eds, erl, neg, sacc, racc, rel, src, dst, rows, *prep = call(
        first_kernel,
        [
            ids, ids, ids, ids,
            ((srows // LANES, LANES), F32),
            ((1, nrel), F32),
            ((nrel, width), F32),
            ((srows, width), F32),
            ((drows + 8, width), F32),
            ((edges, width), F32),
            *prep_shapes,
        ],
        firsts,
        [stack, pltpu.SemaphoreType.DMA((srows // CHUNK,)), pltpu.SemaphoreType.DMA((len(firsts),))],
        hbm=len(firsts),
    )
    half = peer = None
    for step in range(steps):
        last = step == steps - 1
        outs = [
            ((nrel // 2, width), F32),
            ((nrel // 2, width), F32),
            ((2, edges, drows), BF16),
            ((2, edges, width), BF16),
            ((edges, width), F32),
        ]
        if step == 0:
            args = [spot, core, rel, rows, dst, *prep]
        else:
            args = [spot, core, half, peer, racc, rel, rows, dst, *prep]
            outs += [((nrel, width), F32), ((1, nrel), F32)]
        res = call(functools.partial(query_kernel, step, step > 0, nsrc if last else 1), outs, args, smem=2)
        keep, send, wgt, qry, gsr = res[:5]
        if step > 0:
            rel, racc = res[5:]
        come = crossed(send, "dst", 1)
        parts = [head, drows - head + 8] if last else [drows + 8]
        dst = call(dst_kernel, [((n, width), F32) for n in parts], [wgt, qry, dst])
        come, *dst = lax.optimization_barrier((come, *dst))
        dst = [shifted(v, "dst", -(steps - 1) if last else 1) for v in dst]
        half = keep + come
        outs = [((srows, width), F32), ((srows // LANES, LANES), F32)]
        if last:
            size = nrel // 2 // nsrc
            half = half[:size] + sum(
                crossed(half[k * size : (k + 1) * size], "src", k) for k in range(1, nsrc)
            )
            src, sacc = call(
                functools.partial(src_kernel, step, last), outs, [esr, eds, erl, neg, gsr, src, sacc]
            )
            half, src, sacc = lax.optimization_barrier((half, src, sacc))
            half, dst[:1] = exchanged(half, "dst", 2, dst[:1])
            pair = jnp.concatenate([half, crossed(half, "dst", 1)], axis=0)
            pairs = [pair] + [crossed(pair, "src", k) for k in range(1, nsrc)]
        else:
            half = exchanged(half, "src", 1)
            outs += [((edges, width), F32), *prep_shapes]
            res = call(
                functools.partial(src_kernel, step, last), outs, [esr, eds, erl, neg, gsr, src, sacc], [stack]
            )
            half, *res = lax.optimization_barrier((half, *res))
            half, (dst,) = exchanged(half, "dst", 2, dst)
            src, sacc, rows, *prep = res
            peer = crossed(half, "dst", 1)
    rel, racc, dst, dacc = call(
        final_kernel,
        [((nrel, width), F32), ((1, nrel), F32), ((drows, width), F32), ((dblocks, LANES), F32)],
        [core, spot, *pairs, rel, racc, *dst],
        [
            pltpu.VMEM((nrel, width), F32),
            pltpu.VMEM((nrel, width), F32),
            pltpu.VMEM((1, nrel), F32),
            pltpu.SemaphoreType.DMA((5,)),
        ],
        smem=2,
        out_space=pltpu.HBM,
    )
    return src, sacc.reshape(-1), dst, dacc.reshape(-1), rel, racc.reshape(-1)


def solution(mesh):
    both = P(("src", "dst"))
    wide = P(("src", "dst"), None)
    edge = P("src", "dst", None, None, None)
    return jax.shard_map(
        local,
        mesh=mesh,
        in_specs=(wide, both, wide, both, P(), P(), edge, edge, edge, edge),
        out_specs=(wide, both, wide, both, P(), P()),
        check_vma=False,
    )
```

```python
import functools

import jax
import jax.numpy as jnp
from jax import lax
from jax.experimental import pallas as pl
from jax.experimental.pallas import tpu as pltpu
from jax.sharding import PartitionSpec as P

STEPS = 4
RATE = 0.3
EPS = 1e-10
F32 = jnp.float32
BF16 = jnp.bfloat16
LANES = 128
CHUNK = 256
QUERIES = 512


def halves(value):
    high = value.astype(BF16)
    return high, (value - high.astype(F32)).astype(BF16)


def dot(lhs, rhs, lhs_dim=1, rhs_dim=0):
    return lax.dot_general(
        lhs, rhs, (((lhs_dim,), (rhs_dim,)), ((), ())), preferred_element_type=F32
    )


def columns(rows):
    return jnp.transpose(rows)


def hot_columns(cols, first, blocks, width):
    lane = lax.broadcasted_iota(jnp.int32, (LANES, width), 1)
    parts = [
        jnp.where(cols[:, b : b + 1] == lane, 1.0, 0.0).astype(BF16)
        for b in range(first, first + blocks)
    ]
    return jnp.concatenate(parts, axis=0)


def hot_rows(ids, first, blocks, start, height):
    row = lax.broadcasted_iota(jnp.int32, (height, LANES), 0) + start
    parts = [
        jnp.where(row == ids[b : b + 1, :], 1.0, 0.0).astype(BF16)
        for b in range(first, first + blocks)
    ]
    return jnp.concatenate(parts, axis=1)


def row_scale(summed, grad):
    total = summed + jnp.sum(grad * grad, axis=1, keepdims=True) * (1.0 / grad.shape[1])
    return total, RATE / (jnp.sqrt(total) + EPS)


def gather_rows(cols, stack, out_ref, edges, rows):
    blocks = CHUNK // LANES
    for c in range(edges // CHUNK):
        hot = hot_columns(cols, c * blocks, blocks, rows)
        out_ref[c * CHUNK : (c + 1) * CHUNK, :] = dot(jnp.concatenate([hot, hot], axis=1), stack)


def prepare(step, eds_ref, erl_ref, neg_ref, cnt_ref, hit_ref, hot_ref, hot_t_ref):
    blocks, negs = neg_ref.shape[1:]
    rows = cnt_ref.shape[1]
    nrel = hot_t_ref.shape[0]
    cols = columns(neg_ref[step])
    dst_cols = columns(eds_ref[step])
    lane = lax.broadcasted_iota(jnp.int32, (LANES, rows), 1)
    for b in range(blocks):
        found = jnp.where(cols[:, b : b + 1] == lane, 0.5 / negs, 0.0)
        count = jnp.sum(found, axis=0, keepdims=True)
        cnt_ref[b : b + 1, :] = 2.0 * count
        own = jnp.where(dst_cols[:, b : b + 1] == lane, 0.5, 0.0)
        hit_ref[b * LANES : (b + 1) * LANES, :] = own + count
    hot_ref[...] = hot_columns(columns(erl_ref[step]), 0, blocks, nrel)
    hot_t_ref[...] = hot_rows(erl_ref[step], 0, blocks, 0, nrel)


def first_kernel(
    esr_hbm, eds_hbm, erl_hbm, neg_hbm, sac_hbm, dac_hbm, rac_hbm, rel_hbm, src_hbm, dst_hbm,
    esr_ref, eds_ref, erl_ref, neg_ref, sac_ref, rac_ref, rel_ref, src_ref, dst_ref,
    next_ref, cnt_ref, hit_ref, hot_ref, hot_t_ref, stack_ref, src_sem, sem,
):
    rows = src_ref.shape[0]
    drows, width = dst_hbm.shape
    small = [
        pltpu.make_async_copy(source, target, sem.at[k])
        for k, (source, target) in enumerate(
            [
                (neg_hbm, neg_ref),
                (esr_hbm, esr_ref),
                (eds_hbm, eds_ref),
                (erl_hbm, erl_ref),
                (dac_hbm, dst_ref.at[pl.ds(drows, dac_hbm.shape[0]), pl.ds(0, LANES)]),
                (dst_hbm, dst_ref.at[pl.ds(0, drows)]),
                (sac_hbm, sac_ref),
                (rac_hbm, rac_ref),
                (rel_hbm, rel_ref),
            ]
        )
    ]
    for load in small[:4]:
        load.start()
    chunks = rows // CHUNK
    loads = [
        pltpu.make_async_copy(
            src_hbm.at[pl.ds(m * CHUNK, CHUNK)], src_ref.at[pl.ds(m * CHUNK, CHUNK)], src_sem.at[m]
        )
        for m in range(chunks)
    ]
    for load in loads:
        load.start()
    dst_ref[drows : drows + 8, :] = jnp.zeros((8, width), F32)
    for load in small[4:]:
        load.start()
    for load in small[:4]:
        load.wait()
    prepare(0, eds_ref, erl_ref, neg_ref, cnt_ref, hit_ref, hot_ref, hot_t_ref)
    for m in range(chunks):
        loads[m].wait()
        high, low = halves(src_ref[m * CHUNK : (m + 1) * CHUNK, :])
        stack_ref[m * CHUNK : (m + 1) * CHUNK, :] = high
        stack_ref[rows + m * CHUNK : rows + (m + 1) * CHUNK, :] = low
    gather_rows(columns(esr_ref[0]), stack_ref[...], next_ref, next_ref.shape[0], rows)
    for load in small[4:]:
        load.wait()


def both_halves(core_ref, mine_ref, peer_ref):
    first = core_ref[0] == 0
    mine, peer = mine_ref[...], peer_ref[...]
    return jnp.concatenate([jnp.where(first, mine, peer), jnp.where(first, peer, mine)], axis=0)


def relation_update(grad, rel_ref, acc_ref):
    nrel = grad.shape[0]
    total, scale = row_scale(columns(jnp.broadcast_to(acc_ref[...], (8, nrel)))[:, 0:1], grad)
    return rel_ref[...] - grad * scale, columns(jnp.broadcast_to(total, (nrel, LANES)))[0:1, :]


def query_kernel(step, updated, pieces, *refs):
    spot_ref, *refs = refs
    if updated:
        core_ref, mine_ref, peer_ref, acc_ref = refs[:4]
        refs = refs[4:]
    else:
        core_ref = refs[0]
        refs = refs[1:]
    rel_ref, src_ref, dst_ref, cnt_ref, hit_ref, hot_ref, hot_t_ref = refs[:7]
    refs = refs[7:]
    keep_ref, send_ref, wgt_ref, qry_ref, gsr_ref = refs[:5]
    refs = refs[5:]
    if updated:
        rel_out_ref, acc_out_ref = refs
        rel, total = relation_update(both_halves(core_ref, mine_ref, peer_ref), rel_ref, acc_ref)
        rel_out_ref[...] = rel
        acc_out_ref[...] = total
    else:
        rel = rel_ref[...]
    edges = src_ref.shape[0]
    rows = cnt_ref.shape[1]
    nrel = rel.shape[0]
    blocks = QUERIES // LANES
    rel_stack = jnp.concatenate(halves(rel), axis=0)
    dst_high, dst_low = halves(dst_ref[0:rows, :])
    half_high, half_low = 0.5 * dst_high, 0.5 * dst_low
    counts = cnt_ref[...]

    def ask(c):
        at = slice(c * QUERIES, (c + 1) * QUERIES)
        hot = hot_ref[at, :]
        rel_rows = dot(jnp.concatenate([hot, hot], axis=1), rel_stack)
        query = src_ref[at, :] * rel_rows
        q_high, q_low = halves(query)
        qry_ref[0, at, :] = q_high
        qry_ref[1, at, :] = q_low
        scores = (
            dot(q_high, half_high, 1, 1) + dot(q_high, half_low, 1, 1) + dot(q_low, half_high, 1, 1)
        )
        return rel_rows, scores

    def answer(c, rel_rows, scores):
        at = slice(c * QUERIES, (c + 1) * QUERIES)
        slope = jnp.tanh(scores) - 1.0
        parts = []
        for b in range(blocks):
            block = c * blocks + b
            rows_at = slice(block * LANES, (block + 1) * LANES)
            part = slope[b * LANES : (b + 1) * LANES, :]
            parts.append(hit_ref[rows_at, :] * part + counts[block : block + 1, :])
        weight = jnp.concatenate(parts, axis=0)
        w_high, w_low = halves(weight)
        wgt_ref[0, at, :] = w_high
        wgt_ref[1, at, :] = w_low
        grad_query = dot(w_high, dst_high) + dot(w_high, dst_low) + dot(w_low, dst_high)
        gsr_ref[at, :] = grad_query * rel_rows
        return grad_query

    def share(c, grad_query):
        at = slice(c * QUERIES, (c + 1) * QUERIES)
        hot_t = hot_t_ref[:, at]
        return dot(
            jnp.concatenate([hot_t, hot_t], axis=1),
            jnp.concatenate(halves(grad_query * src_ref[at, :]), axis=0),
        )

    count = edges // QUERIES
    grad = None
    asked = ask(0)
    for c in range(count):
        ready = asked
        if c + 1 < count:
            asked = ask(c + 1)
        part = share(c, answer(c, *ready))
        grad = part if grad is None else grad + part
    first = core_ref[0] == 0
    half = nrel // 2
    top, bottom = grad[:half], grad[half:]
    keep = jnp.where(first, top, bottom)
    send = jnp.where(first, bottom, top)
    size = half // pieces
    for m in range(pieces):
        at = pl.ds(pl.multiple_of((spot_ref[0] ^ m) * size, size), size) if pieces > 1 else slice(0, half)
        keep_ref[at, :] = keep[m * size : (m + 1) * size]
        send_ref[at, :] = send[m * size : (m + 1) * size]


def dst_kernel(wgt_ref, qry_ref, dst_ref, *outs):
    rows = wgt_ref.shape[2]
    width = dst_ref.shape[1]
    head = 0 if len(outs) == 1 else outs[0].shape[0]
    tail_ref = outs[-1]
    wide = dot(wgt_ref[0], jnp.concatenate([qry_ref[0], qry_ref[1]], axis=1), 0, 0)
    grad = wide[:, :width] + wide[:, width:] + dot(wgt_ref[1], qry_ref[0], 0, 0)
    blocks = rows // LANES
    cols = columns(dst_ref[rows : rows + 8, 0:LANES])
    totals = []
    for b in range(blocks):
        at = slice(b * LANES, (b + 1) * LANES)
        total, scale = row_scale(cols[:, b : b + 1], grad[at])
        totals.append(total)
        fresh = dst_ref[at, :] - grad[at] * scale
        if b * LANES < head:
            outs[0][at, :] = fresh
        else:
            tail_ref[b * LANES - head : (b + 1) * LANES - head, :] = fresh
    sums = jnp.transpose(jnp.concatenate(totals + [totals[0]] * (8 - blocks), axis=1))
    tail_ref[rows - head : rows - head + 8, :] = jnp.concatenate(
        [sums, jnp.zeros((8, width - LANES), F32)], axis=1
    )


def src_kernel(step, last, esr_ref, eds_ref, erl_ref, neg_ref, gsr_ref, src_ref, acc_ref, *refs):
    if last:
        src_out_ref, acc_out_ref = refs
    else:
        src_out_ref, acc_out_ref, next_ref, *prep, stack_ref = refs
    rows = src_ref.shape[0]
    edges = gsr_ref.shape[0]
    gsr = jnp.concatenate(halves(gsr_ref[...]), axis=0)
    cols = columns(acc_ref[...])
    totals = []
    for m in range(rows // CHUNK):
        at = slice(m * CHUNK, (m + 1) * CHUNK)
        hot_t = hot_rows(esr_ref[step], 0, edges // LANES, m * CHUNK, CHUNK)
        grad = dot(jnp.concatenate([hot_t, hot_t], axis=1), gsr)
        summed = jnp.concatenate(
            [
                cols[:, b : b + 1]
                for b in range(m * CHUNK // LANES, (m + 1) * CHUNK // LANES)
            ],
            axis=0,
        )
        total, scale = row_scale(summed, grad)
        fresh = src_ref[at, :] - grad * scale
        src_out_ref[at, :] = fresh
        for b in range(CHUNK // LANES):
            totals.append(total[b * LANES : (b + 1) * LANES])
        if not last:
            high, low = halves(fresh)
            stack_ref[at, :] = high
            stack_ref[rows + m * CHUNK : rows + (m + 1) * CHUNK, :] = low
    acc_out_ref[...] = jnp.transpose(jnp.concatenate(totals, axis=1))
    if not last:
        gather_rows(columns(esr_ref[step + 1]), stack_ref[...], next_ref, edges, rows)
        prepare(step + 1, eds_ref, erl_ref, neg_ref, *prep)


def final_kernel(core_ref, spot_ref, *refs):
    pairs = refs[:-12]
    rel_ref, acc_ref, head_ref, tail_ref = refs[-12:-8]
    rel_out, acc_out, dst_out, dac_out, grad_ref, rel_buf, acc_buf, sem = refs[-8:]
    head = head_ref.shape[0]
    rest = dst_out.shape[0] - head
    moves = [
        pltpu.make_async_copy(source, target, sem.at[k])
        for k, (source, target) in enumerate(
            [
                (head_ref, dst_out.at[pl.ds(0, head)]),
                (tail_ref.at[pl.ds(0, rest)], dst_out.at[pl.ds(head, rest)]),
                (tail_ref.at[pl.ds(rest, dac_out.shape[0]), pl.ds(0, LANES)], dac_out),
                (rel_buf, rel_out),
                (acc_buf, acc_out),
            ]
        )
    ]
    for move in moves[:3]:
        move.start()
    rows = pairs[0].shape[0] // 2
    half = grad_ref.shape[0] // 2
    core = core_ref[0]
    for k, pair_ref in enumerate(pairs):
        at = (spot_ref[0] ^ k) * rows
        mine = pl.multiple_of(core * half + at, rows)
        peer = pl.multiple_of((1 - core) * half + at, rows)
        grad_ref[pl.ds(mine, rows), :] = pair_ref[0:rows, :]
        grad_ref[pl.ds(peer, rows), :] = pair_ref[rows : 2 * rows, :]
    rel, total = relation_update(grad_ref[...], rel_ref, acc_ref)
    rel_buf[...] = rel
    acc_buf[...] = total
    for move in moves[3:]:
        move.start()
    for move in moves:
        move.wait()


def call(body, outs, args, scratch=(), smem=0, hbm=0, out_space=pltpu.VMEM):
    spaces = [pltpu.SMEM] * smem + [pltpu.VMEM] * (len(args) - smem - hbm) + [pltpu.HBM] * hbm
    in_specs = [pl.BlockSpec(memory_space=space) for space in spaces]
    return pl.pallas_call(
        body,
        out_shape=tuple(jax.ShapeDtypeStruct(s, d) for s, d in outs),
        in_specs=in_specs,
        out_specs=tuple(pl.BlockSpec(memory_space=out_space) for _ in outs),
        scratch_shapes=list(scratch),
        compiler_params=pltpu.CompilerParams(vmem_limit_bytes=40 << 20),
    )(*args[: len(args) - hbm], *[pltpu.with_memory_space_constraint(v, pltpu.HBM) for v in args[len(args) - hbm :]])


def shifted(value, axis, steps):
    count = lax.axis_size(axis)
    return lax.ppermute(value, axis, [(k, (k + steps) % count) for k in range(count)])


def crossed(value, axis, bits):
    count = lax.axis_size(axis)
    return lax.ppermute(value, axis, [(k, k ^ bits) for k in range(count)])


def exchanged(value, axis, low, late=None):
    count = lax.axis_size(axis)
    while low < count:
        reach = min(4, count // low)
        last = value
        if late is not None:
            last, late = lax.optimization_barrier((value, late))
        come = [crossed(last if k == 1 else value, axis, low * k) for k in range(1, reach)]
        value = sum(come, value)
        low *= reach
        if late is not None:
            return exchanged(value, axis, low), late
    return value


def local(
    src_emb, src_acc, dst_emb, dst_acc, rel_emb, rel_acc, edge_src, edge_dst, edge_rel, negatives
):
    esr, eds, erl, neg = (v[0, 0] for v in (edge_src, edge_dst, edge_rel, negatives))
    steps, eblocks, _ = esr.shape
    edges = eblocks * LANES
    srows, width = src_emb.shape
    drows = dst_emb.shape[0]
    nrel = rel_emb.shape[0]
    core = (lax.axis_index("dst") & 1).astype(jnp.int32).reshape(1)
    spot = lax.axis_index("src").astype(jnp.int32).reshape(1)
    nsrc = lax.axis_size("src")
    head = (drows // LANES // 2) * LANES
    sacc = src_acc.reshape(srows // LANES, LANES)
    dblocks = drows // LANES
    stack = pltpu.VMEM((2 * srows, width), BF16)
    ids = (esr.shape, jnp.int32)
    prep_shapes = [
        ((eblocks, drows), F32),
        ((edges, drows), F32),
        ((edges, nrel), BF16),
        ((nrel, edges), BF16),
    ]
    firsts = [
        esr, eds, erl, neg, sacc, dst_acc.reshape(dblocks, LANES), rel_acc.reshape(1, nrel),
        rel_emb, src_emb, dst_emb,
    ]
    esr, eds, erl, neg, sacc, racc, rel, src, dst, rows, *prep = call(
        first_kernel,
        [
            ids, ids, ids, ids,
            ((srows // LANES, LANES), F32),
            ((1, nrel), F32),
            ((nrel, width), F32),
            ((srows, width), F32),
            ((drows + 8, width), F32),
            ((edges, width), F32),
            *prep_shapes,
        ],
        firsts,
        [stack, pltpu.SemaphoreType.DMA((srows // CHUNK,)), pltpu.SemaphoreType.DMA((len(firsts),))],
        hbm=len(firsts),
    )
    half = peer = None
    for step in range(steps):
        last = step == steps - 1
        outs = [
            ((nrel // 2, width), F32),
            ((nrel // 2, width), F32),
            ((2, edges, drows), BF16),
            ((2, edges, width), BF16),
            ((edges, width), F32),
        ]
        if step == 0:
            args = [spot, core, rel, rows, dst, *prep]
        else:
            args = [spot, core, half, peer, racc, rel, rows, dst, *prep]
            outs += [((nrel, width), F32), ((1, nrel), F32)]
        res = call(functools.partial(query_kernel, step, step > 0, nsrc if last else 1), outs, args, smem=2)
        keep, send, wgt, qry, gsr = res[:5]
        if step > 0:
            rel, racc = res[5:]
        come = crossed(send, "dst", 1)
        parts = [head, drows - head + 8] if last else [drows + 8]
        dst = call(dst_kernel, [((n, width), F32) for n in parts], [wgt, qry, dst])
        come, *dst = lax.optimization_barrier((come, *dst))
        dst = [shifted(v, "dst", -(steps - 1) if last else 1) for v in dst]
        half = keep + come
        outs = [((srows, width), F32), ((srows // LANES, LANES), F32)]
        if last:
            size = nrel // 2 // nsrc
            half = half[:size] + sum(
                crossed(half[k * size : (k + 1) * size], "src", k) for k in range(1, nsrc)
            )
            src, sacc = call(
                functools.partial(src_kernel, step, last), outs, [esr, eds, erl, neg, gsr, src, sacc]
            )
            half, src, sacc = lax.optimization_barrier((half, src, sacc))
            half, dst[:1] = exchanged(half, "dst", 2, dst[:1])
            pair = jnp.concatenate([half, crossed(half, "dst", 1)], axis=0)
            pairs = [pair] + [crossed(pair, "src", k) for k in range(1, nsrc)]
        else:
            half = exchanged(half, "src", 1)
            outs += [((edges, width), F32), *prep_shapes]
            res = call(
                functools.partial(src_kernel, step, last), outs, [esr, eds, erl, neg, gsr, src, sacc], [stack]
            )
            half, *res = lax.optimization_barrier((half, *res))
            half, (dst,) = exchanged(half, "dst", 2, dst)
            src, sacc, rows, *prep = res
            peer = crossed(half, "dst", 1)
    rel, racc, dst, dacc = call(
        final_kernel,
        [((nrel, width), F32), ((1, nrel), F32), ((drows, width), F32), ((dblocks, LANES), F32)],
        [core, spot, *pairs, rel, racc, *dst],
        [
            pltpu.VMEM((nrel, width), F32),
            pltpu.VMEM((nrel, width), F32),
            pltpu.VMEM((1, nrel), F32),
            pltpu.SemaphoreType.DMA((5,)),
        ],
        smem=2,
        out_space=pltpu.HBM,
    )
    return src, sacc.reshape(-1), dst, dacc.reshape(-1), rel, racc.reshape(-1)


def solution(mesh):
    both = P(("src", "dst"))
    wide = P(("src", "dst"), None)
    edge = P("src", "dst", None, None, None)
    return jax.shard_map(
        local,
        mesh=mesh,
        in_specs=(wide, both, wide, both, P(), P(), edge, edge, edge, edge),
        out_specs=(wide, both, wide, both, P(), P()),
        check_vma=False,
    )
```
